256 devices in a mesh: seq: 8 (over x, core), clus: 32 (over y, z).
Axes of the slice: x: 4, y: 4, z: 8, core: 2. Of those that a mesh axis runs over, the one named last changes fastest.
Arguments:
- features: bfloat16 [32768, 1024], P(('seq', 'clus')), may hold values from -6 to 6
- shortlist: int32 [32768, 16], P(('seq', 'clus')), may hold values from 0 to 255, all different within a row; in each aligned block of 128 rows (0 to 127, 128 to 255, ...) at most 10 rows name the same one
- positives: int32 [32768, 4], P(('seq', 'clus')), may hold values from 0 to 2047
- cluster_sizes: int32 [256], P('clus'), may hold values from 1 to 128, 24576 in all
- weights: bfloat16 [32768, 1024], P('clus'), may hold values from -0.1875 to 0.1875
Outputs:
- feature_grad: bfloat16 [32768, 1024], P(('seq', 'clus'))
- weight_grad: bfloat16 [32768, 1024], P('clus', 'seq')
The draws below stay inside these ranges and needn't reach their ends.
Inputs may be any that keep to these rules, and one draw needn't show every extreme that they name: `shortlist`: the 16 ids of a row are distinct; within the rows of one device (aligned blocks of 128 rows) no cluster is named by more than 10 rows, a bound that some block reaches. `positives`: a value q names offset q % 128 of the cluster at shortlist place q // 128; values may repeat, and offsets at or past that cluster's size name nothing. `cluster_sizes`: some cluster has exactly 128 labels.
All inputs are finite; a program needn't handle non-finite values.
Results may differ from the reference program's by a relative error of at most 0.018.
Values may be sent and summed in bfloat16 or wider, within the bound.
A program may use at most 64 MiB of HBM per device.

```python
import math
import jax
import jax.numpy as jnp
import numpy as np
from jax import lax

D = 1024
BLOCK = 128
TOP = 16
NPOS = 4
INST_DEV = 128
INSTANCES = 32768
CLUSTERS = 256
LABELS = 32768
MOST = 10
PAIRS_CL = 2048
N_SEQ = 8
N_CLUS = 32


def set_ends(values, rng, smallest, top_value):
    shape = values.shape
    index_at = [jax.random.randint(jax.random.fold_in(rng, axis), (), 0, shape[axis]) for axis in range(len(shape))]
    values = values.at[tuple(index_at)].set(smallest)
    longest = shape.index(max(shape))
    index_at[longest] = (index_at[longest] + 1) % shape[longest]
    return values.at[tuple(index_at)].set(top_value)


def steps_of(own_key, extent, split, least, top_value):
    loudness, own = 1.0, jax.random.fold_in(own_key, 6)
    for axis_at, shards_of in split:
        steps = jnp.exp(jax.random.uniform(jax.random.fold_in(own, axis_at), (shards_of,), jnp.float32, least / len(split), top_value / len(split)))
        loudness = loudness * jnp.repeat(steps, extent[axis_at] // shards_of).reshape([-1 if axis == axis_at else 1 for axis in range(len(extent))])
    return loudness


def split_up(amount, total, limit, slope):
    portions = [(1 << 20) // math.isqrt(standing ** slope) + 1 for standing in range(2, amount + 1)]
    surplus, given = total - limit - (amount - 1), [1] * (amount - 1)
    while surplus > 0:
        movable = [i for i in range(amount - 1) if given[i] < limit]
        pool, budget = sum([portions[i] for i in movable]), surplus
        for i in movable:
            extra = min(limit - given[i], max(1, budget * portions[i] // pool), surplus)
            given[i] = given[i] + extra
            surplus = surplus - extra
    return np.array([limit] + given)


def ragged(key, amount, total, bound, lean):
    if amount == 2:
        one = jax.random.randint(key, (), max(1, total - bound), min(bound, total - 1) + 1)
        return jnp.stack([one, total - one])
    tallies = jnp.asarray(split_up(amount, total, bound, lean), jnp.int32)
    twos = (amount - 1) // 2
    giver, taker = tallies[1:1 + 2 * twos:2], tallies[2:2 + 2 * twos:2]
    margin = jnp.minimum(giver - 1, bound - taker)
    moved = jax.random.randint(jax.random.fold_in(key, 1), (twos,), 0, 1 << 20) % (margin + 1)
    tallies = tallies.at[1:1 + 2 * twos:2].set(giver - moved).at[2:2 + 2 * twos:2].set(taker + moved)
    return tallies[jax.random.permutation(jax.random.fold_in(key, 2), amount)]


def assign_block(rng, own, number, rows, amount, top, reach, slope):
    order = jax.random.permutation(rng, amount)
    heavy_load, usual = shares(amount, rows * top, reach, slope, True), shares(amount, rows * top, reach, slope, False)
    places = jnp.arange(amount)

    def named(tallies, rotation):
        used = int((tallies > 0).sum())
        fixed = max(1, used // 4)
        shifted = fixed + (places - fixed + rotation * (used - fixed)) % max(1, amount - fixed)
        return jnp.zeros((amount,), jnp.int32).at[order[jnp.where(places < fixed, places, shifted)]].set(jnp.asarray(tallies, jnp.int32))

    tallies = jnp.where(number % 4 == 0, named(heavy_load, number // 4), named(usual, number - number // 4 - 1))
    mixed = jax.random.permutation(jax.random.fold_in(own, 3), amount)
    giver, taker = mixed[0:amount // 2 * 2:2], mixed[1:amount // 2 * 2:2]
    margin = jnp.minimum(tallies[giver] - 1, reach - tallies[taker]) // 2
    margin = jnp.where((giver == order[0]) | (taker == order[0]) | (tallies[taker] == 0), 0, jnp.maximum(margin, 0))
    shifted = jax.random.randint(jax.random.fold_in(own, 4), (amount // 2,), 0, 1 << 20) % (margin + 1)
    tallies = tallies.at[giver].add(-shifted).at[taker].add(shifted)
    members = jnp.searchsorted(jnp.cumsum(tallies), jnp.arange(rows * top), side="right").astype(jnp.int32)
    table = members.reshape(top, rows).T
    table = table[jax.random.permutation(jax.random.fold_in(own, 1), rows)]
    rotation = jax.random.randint(jax.random.fold_in(own, 2), (rows, 1), 0, top)
    return jnp.take_along_axis(table, (jnp.arange(top)[None, :] + rotation) % top, axis=1)


def shares(amount, total, bound, slope, full):
    loads = [(1 << 20) // math.isqrt(rank ** slope) + 1 for rank in range(1, amount + 1)]
    largest = bound if full else min(bound, max(-(-total // amount), total * loads[0] // sum(loads)))
    least = 1 if total - largest >= amount - 1 else 0
    counts, rest = [largest] + [least] * (amount - 1), total - largest - least * (amount - 1)
    while rest > 0:
        free = [i for i in range(1, amount) if counts[i] < largest] or [i for i in range(1, amount) if counts[i] < bound]
        mass, left = sum([loads[i] for i in free]), rest
        for i in free:
            addition = min(bound - counts[i], max(1, left * loads[i] // mass), rest)
            counts[i] = counts[i] + addition
            rest = rest - addition
    return np.array(counts)


def normal_values(rng, shape, width, limit, pieces=(), kind=jnp.bfloat16):
    factor_of = steps_of(rng, shape, pieces, -0.22, 0.18) if pieces else 1.0
    values = jax.random.normal(rng, shape, jnp.float32) * width * factor_of
    return jnp.minimum(jnp.maximum(values, -limit), limit).astype(kind)


def setup_inputs(seed: int = 0) -> dict:
    keys = jax.random.split(jax.random.key(seed), 6)
    features = normal_values(keys[0], (INSTANCES, D), 1.0, 6.0, ((0, 256),))
    shortlist_keys = jax.random.split(jax.random.fold_in(keys[1], 1), INSTANCES // INST_DEV)
    shortlist_turns = jax.random.permutation(jax.random.fold_in(keys[1], 3), INSTANCES // INST_DEV)
    shortlist = jax.vmap(lambda own, number: assign_block(jax.random.fold_in(keys[1], 2), own, number, INST_DEV, CLUSTERS, TOP, MOST, 2))(shortlist_keys, shortlist_turns).reshape((INSTANCES, TOP))
    positives = set_ends(jax.random.randint(keys[2], (INSTANCES, NPOS), 0, TOP * BLOCK), jax.random.fold_in(keys[2], 1), 0, (TOP * BLOCK) - 1).astype(jnp.int32)
    cluster_sizes = ragged(keys[3], CLUSTERS, CLUSTERS * 96, BLOCK, 1).astype(jnp.int32)
    weights = normal_values(keys[4], (LABELS, D), D ** -0.5, 0.1875, ((0, 32),))
    return dict(features=features, shortlist=shortlist, positives=positives, cluster_sizes=cluster_sizes, weights=weights)


def reference(features, shortlist, positives, cluster_sizes, weights):
    group_rows = INST_DEV * N_CLUS
    slot_count = N_CLUS * MOST
    cluster_ids = jnp.arange(CLUSTERS, dtype=jnp.int32)
    label_ids = jnp.arange(BLOCK, dtype=jnp.int32)

    def ranks_of(short_block):
        member = lax.optimization_barrier(jnp.sum((short_block[:, :, None] == cluster_ids[None, None, :]).astype(jnp.int32), axis=1))
        ranking = jnp.cumsum(member, axis=0) - member
        return jnp.take_along_axis(ranking, short_block, axis=1)
    pair_rank = lax.map(ranks_of, shortlist.reshape(-1, INST_DEV, TOP)).reshape(INSTANCES, TOP)
    within = jnp.arange(INSTANCES, dtype=jnp.int32) // INST_DEV % N_CLUS
    slot_table = within[:, None] * MOST + pair_rank
    weight_table = weights.reshape(CLUSTERS, BLOCK, D)
    norm_scale = 1.0 / math.sqrt(PAIRS_CL)

    def per_group(running, group_index):
        start = (group_index * group_rows).astype(jnp.int32)
        feat_group = lax.dynamic_slice_in_dim(features, start, group_rows, 0)
        short_group = lax.dynamic_slice_in_dim(shortlist, start, group_rows, 0)
        pos_group = lax.dynamic_slice_in_dim(positives, start, group_rows, 0)
        slot_group = lax.dynamic_slice_in_dim(slot_table, start, group_rows, 0)
        local_index = jnp.broadcast_to(jnp.arange(group_rows, dtype=jnp.int32)[:, None], (group_rows, TOP))
        short_place = jnp.broadcast_to(jnp.arange(TOP, dtype=jnp.int32)[None, :], (group_rows, TOP))
        slot_owner = jnp.zeros((CLUSTERS, slot_count), jnp.int32).at[short_group, slot_group].set(local_index)
        slot_place = jnp.zeros((CLUSTERS, slot_count), jnp.int32).at[short_group, slot_group].set(short_place)
        slot_filled = jnp.zeros((CLUSTERS, slot_count), jnp.int32).at[short_group, slot_group].set(1)

        def per_cluster(cluster):
            owner_row = slot_owner[cluster]
            filled = slot_filled[cluster]
            tile_rows = feat_group[owner_row] * filled[:, None].astype(jnp.bfloat16)
            pos_rows = pos_group[owner_row]
            matches = (pos_rows // BLOCK == slot_place[cluster][:, None]) & (filled[:, None] > 0)
            targets = jnp.where(matches, pos_rows % BLOCK, -1)
            block_weights = weight_table[cluster]
            logits = jnp.dot(tile_rows, block_weights.T, preferred_element_type=jnp.float32)
            positive = jnp.any(targets[:, :, None] == label_ids[None, None, :], axis=1)
            target_sign = jnp.where(positive, 1.0, -1.0)
            live_entry = (label_ids[None, :] < cluster_sizes[cluster]) & (filled[:, None] > 0)
            hinge_slope = jnp.where(live_entry, -2.0 * target_sign * jnp.maximum(1.0 - target_sign * logits, 0.0), 0.0).astype(jnp.bfloat16)
            pair_grads = jnp.dot(hinge_slope, block_weights, preferred_element_type=jnp.float32).astype(jnp.bfloat16)
            label_part = jnp.dot(hinge_slope.T, tile_rows, preferred_element_type=jnp.float32).astype(jnp.bfloat16)
            return (pair_grads, label_part)
        pair_grads, label_part = lax.map(per_cluster, cluster_ids)
        picked = pair_grads[short_group, slot_group]
        feature_rows = lax.optimization_barrier(jnp.sum(picked.astype(jnp.float32), axis=1)).astype(jnp.bfloat16)
        label_part = lax.optimization_barrier(label_part)
        running = running + label_part.reshape(LABELS, D).astype(jnp.float32)
        return (running, feature_rows)
    running, feature_blocks = lax.scan(per_group, jnp.zeros((LABELS, D), jnp.float32), jnp.arange(N_SEQ, dtype=jnp.int32))
    weight_grad = (running * norm_scale).astype(jnp.bfloat16)
    return (feature_blocks.reshape(INSTANCES, D), weight_grad)
```

```python
import math

import jax
import jax.numpy as jnp
from jax import lax
from jax.experimental import pallas as pl
from jax.experimental.pallas import tpu as pltpu
from jax.sharding import PartitionSpec as P

MESH = pl.DeviceIdType.MESH
NX, NY, NZ = 4, 4, 8
BLK = 128
SLOTS = 16
NB = 16
NK = 16
D = 1024
CT = 256
F32, BF16 = jnp.float32, jnp.bfloat16


def slot_of(dz, dc):
    hop = min(dz, NZ - dz)
    if hop == 0:
        return dc
    if hop == NZ // 2:
        return NB - 2 + dc
    return 4 * hop - 2 + (0 if dz < NZ // 2 else 1) + 2 * dc


def nt_dot(a, b):
    return lax.dot_general(a, b, (((1,), (1,)), ((), ())), preferred_element_type=F32)


def nn_dot(a, b):
    return jnp.dot(a, b, preferred_element_type=F32)


def body(
    scale, f_in, sl_in, pos_in, sz_in, w_in, df_out, wg_out,
    F, M, W, SZ, X, PGB, TG, PM, PT, LP, XS, XR1, XR2, RB, RF, YS, YR1, YR2, SB, SBR,
    DP, DS, EF, ZS, ZR, send_sems, recv_sems, local_sems,
):
    s, q = lax.axis_index("seq"), lax.axis_index("clus")
    x, c, y, z = s // 2, s % 2, q // NZ, q % NZ
    sib = (s + 1 - 2 * c, q)
    to_x = {1: ((s + 2) % 8, q), -1: ((s + 6) % 8, q)}
    to_y = {1: (s, (q + 8) % 32), -1: (s, (q + 24) % 32)}
    to_z = {1: (s, y * 8 + (z + 1) % 8), -1: (s, y * 8 + (z + 7) % 8)}
    partners = [sib, *to_x.values(), *to_y.values(), *to_z.values()]
    sent, arrived = [], set()

    def arrive(copy):
        if id(copy) not in arrived:
            arrived.add(id(copy))
            copy.wait_recv()

    def message(src, dst, device):
        number = len(sent)
        copy = pltpu.make_async_remote_copy(
            src_ref=src, dst_ref=dst, send_sem=send_sems.at[number], recv_sem=recv_sems.at[number],
            device_id=device, device_id_type=MESH,
        )
        copy.start()
        sent.append(copy)
        return copy

    cp_f = pltpu.make_async_copy(f_in, F.at[0], local_sems.at[0])
    cp_w = pltpu.make_async_copy(w_in.at[pl.ds(4 * c, 4)], W.at[0], local_sems.at[1])
    cp_f.start()
    cp_w.start()
    barrier = pltpu.get_barrier_semaphore()
    for device in partners:
        pl.semaphore_signal(barrier, inc=1, device_id=device, device_id_type=MESH)

    short = sl_in[...]
    place_row = lax.broadcasted_iota(jnp.int32, (16, BLK), 0)
    pos_cl = jnp.full((16, BLK), -1.0, F32)
    pos_off = jnp.full((16, BLK), -1.0, F32)
    for j in range(4):
        code = pos_in[j : j + 1, :]
        named = jnp.sum(jnp.where(place_row == (code >> 7), short, 0), axis=0, keepdims=True)
        pos_cl = jnp.where(place_row == j, named.astype(F32), pos_cl)
        pos_off = jnp.where(place_row == j, (code & 127).astype(F32), pos_off)
    M[0, 0:16, :] = short.astype(F32).astype(BF16)
    M[0, 16:32, :] = pos_cl.astype(BF16)
    M[0, 32:48, :] = pos_off.astype(BF16)
    row8 = lax.broadcasted_iota(jnp.int32, (8, BLK), 0)
    sizes = jnp.zeros((8, BLK), F32)
    for k in range(4):
        sizes = jnp.where(row8 == k, sz_in[4 * c + k].astype(F32), sizes)
    SZ[0] = sizes

    pl.semaphore_wait(barrier, len(partners))

    HALF = {"A": pl.ds(0, 64), "B": pl.ds(64, 64)}

    def landing(h, way):
        return h if way < 0 else NZ - h

    f_msg, m_msg, sf_msg, sm_msg = {}, {}, {}, {}

    def halves(h, way):
        if h == 4:
            return ["A"] if way < 0 else ["B"]
        return ["A", "B"] if way < 0 else ["B", "A"]

    def send_half(h, way, half):
        src = slot_of(landing(h - 1, way) % NZ, 0)
        dst = slot_of(landing(h, way), 0)
        f_msg[h, way, half] = message(F.at[src, HALF[half]], F.at[dst, HALF[half]], to_z[way])

    def send_meta(h, way):
        src = slot_of(landing(h - 1, way) % NZ, 0)
        dst = slot_of(landing(h, way), 0)
        m_msg[h, way] = message(M.at[src], M.at[dst], to_z[way])

    def share_half(dz, half):
        sf_msg[dz, half] = message(
            F.at[slot_of(dz, 0), HALF[half]], F.at[slot_of(dz, 1), HALF[half]], sib
        )

    def share_meta(dz):
        sm_msg[dz] = message(M.at[slot_of(dz, 0)], M.at[slot_of(dz, 1)], sib)

    w_msg, z_msg = {}, {}

    for way in (-1, 1):
        send_meta(1, way)
    share_meta(0)
    cp_f.wait()
    for i in range(2):
        for way in (-1, 1):
            send_half(1, way, halves(1, way)[i])
    share_half(0, "A")
    share_half(0, "B")
    z_msg[1] = message(SZ.at[0], SZ.at[1], to_y[-1])
    z_msg[3] = message(SZ.at[0], SZ.at[3], to_y[1])
    cp_w.wait()
    for i in range(4):
        k = i
        w_msg[1, k] = message(W.at[0, k], W.at[1, k], to_y[-1])
        k = (i + 2) % 4
        w_msg[3, k] = message(W.at[0, k], W.at[3, k], to_y[1])

    def relay_weights(i):
        arrive(w_msg[1, i])
        w_msg[2, i] = message(W.at[1, i], W.at[2, i], to_y[-1])
        arrive(w_msg[3, 2 + i])
        w_msg[2, 2 + i] = message(W.at[3, 2 + i], W.at[2, 2 + i], to_y[1])

    kk16 = lax.broadcasted_iota(jnp.int32, (16, BLK), 0)
    cid16 = (((((y + (kk16 >> 2)) & 3) * 8 + z) * 8) + 4 * c + (kk16 & 3)).astype(F32)
    kk256 = lax.broadcasted_iota(jnp.int32, (256, 16), 0) >> 4
    cid256 = (((((y + (kk256 >> 2)) & 3) * 8 + z) * 8) + 4 * c + (kk256 & 3)).astype(F32)
    slot_row = lax.broadcasted_iota(jnp.int32, (16, BLK), 0).astype(F32)

    def pick(b):
        names = M[b, 0:16, :].astype(F32)
        member = jnp.zeros((16, BLK), F32)
        for j in range(16):
            member = member + jnp.where(names[j : j + 1, :] == cid16, 1.0, 0.0)
        before = (
            lax.broadcasted_iota(jnp.int32, (BLK, BLK), 0)
            < lax.broadcasted_iota(jnp.int32, (BLK, BLK), 1)
        )
        rank = nn_dot(member.astype(BF16), jnp.where(before, 1.0, 0.0).astype(BF16))
        rank = jnp.where(member > 0.0, rank, -1.0)
        for k in range(NK):
            PM[b, k * 16 : (k + 1) * 16, :] = jnp.where(
                rank[k : k + 1, :] == slot_row, 1.0, 0.0
            ).astype(BF16)
        picks = PM[b]
        PT[b] = jnp.transpose(picks.astype(F32)).astype(BF16)
        named = nt_dot(picks, M[b, 16:32, :])
        offset = nt_dot(picks, M[b, 32:48, :])
        TG[:, b] = jnp.where(named == cid256, offset, -1.0).reshape(16, 16, 16)
        for n in range(D // CT):
            cols = slice(n * CT, (n + 1) * CT)
            X[:, b, :, cols] = nn_dot(picks, F[b, :, cols]).astype(BF16).reshape(16, 16, CT)

    def pick_range(first, count):
        lax.fori_loop(0, count, lambda i, _: (pick(first + i), 0)[1], 0)

    def await_shared(dz):
        arrive(sm_msg[dz])
        arrive(sf_msg[dz, "A"])
        arrive(sf_msg[dz, "B"])

    pick_range(0, 1)
    for h in range(1, 5):
        for i in range(2 if h < 4 else 1):
            for way in (-1, 1):
                half = halves(h, way)[i]
                arrive(f_msg[h, way, half])
                if h < 4 and half in halves(h + 1, way):
                    send_half(h + 1, way, half)
            for way in (-1, 1):
                half = halves(h, way)[i]
                share_half(landing(h, way), half)
        for way in (-1, 1):
            if h < 4 or way < 0:
                arrive(m_msg[h, way])
                if h < 3 or (h == 3 and way < 0):
                    send_meta(h + 1, way)
                share_meta(landing(h, way))
        if h in (1, 2):
            relay_weights(h - 1)
            if h == 1:
                arrive(z_msg[1])
                z_msg[2] = message(SZ.at[1], SZ.at[2], to_y[-1])
        if h < 4:
            pick_range(4 * h - 2, 2)
        else:
            pick_range(14, 1)
        if h == 1:
            await_shared(0)
            pick_range(1, 1)
        else:
            await_shared(h - 1)
            await_shared(NZ - h + 1)
            pick_range(4 * (h - 1), 2)
    await_shared(4)
    pick_range(15, 1)

    lane = lax.broadcasted_iota(jnp.int32, (256, BLK), 1).astype(F32)

    def cluster(dy, k):
        kk = 4 * dy + k
        weights = W[dy, k]
        logits = nt_dot(X[kk].reshape(256, D), weights)
        target = TG[kk].reshape(256, 16)
        positive = target[:, 0:1] == lane
        for j in range(1, 4):
            positive = positive | (target[:, j : j + 1] == lane)
        sign = jnp.where(positive, 1.0, -1.0)
        live = lane < SZ[dy, pl.ds(k, 1), :]
        slope = jnp.where(live, -2.0 * sign * jnp.maximum(1.0 - sign * logits, 0.0), 0.0)
        turned = jnp.transpose(slope).astype(BF16)
        slope = slope.astype(BF16)
        for dx in range(NX):
            cols = pl.ds(pl.multiple_of(CT * ((x + dx) % NX), CT), CT)
            part = nn_dot(turned, X[kk, :, :, cols].reshape(256, CT))
            LP[dx, dy, k] = part.astype(BF16)
        for n in range(D // CT):
            cols = slice(n * CT, (n + 1) * CT)
            PGB[:, kk, :, cols] = nn_dot(slope, W[dy, k, :, cols]).astype(BF16).reshape(16, 16, CT)

    def clusters(dy):
        lax.fori_loop(0, 4, lambda k, _: (cluster(dy, k), 0)[1], 0)

    LOW, HIGH = pl.ds(0, 2), pl.ds(2, 2)
    x_msg, y_msg = {}, {}

    def x_first(dy):
        x_msg[dy, 1, "far"] = message(LP.at[2, dy, LOW], XR1.at[0, dy], to_x[1])
        x_msg[dy, -1, "far"] = message(LP.at[2, dy, HIGH], XR1.at[1, dy], to_x[-1])
        x_msg[dy, 1, "raw"] = message(LP.at[1, dy, HIGH], XR2.at[0, dy, HIGH], to_x[1])
        x_msg[dy, -1, "raw"] = message(LP.at[3, dy, LOW], XR2.at[1, dy, LOW], to_x[-1])

    def x_second(dy):
        arrive(x_msg[dy, 1, "far"])
        XS[0, dy] = (LP[1, dy, 0:2].astype(F32) + XR1[0, dy].astype(F32)).astype(BF16)
        x_msg[dy, 1, "sum"] = message(XS.at[0, dy], XR2.at[0, dy, LOW], to_x[1])
        arrive(x_msg[dy, -1, "far"])
        XS[1, dy] = (LP[3, dy, 2:4].astype(F32) + XR1[1, dy].astype(F32)).astype(BF16)
        x_msg[dy, -1, "sum"] = message(XS.at[1, dy], XR2.at[1, dy, HIGH], to_x[-1])

    def x_last(dy):
        for way in (1, -1):
            arrive(x_msg[dy, way, "raw"])
            arrive(x_msg[dy, way, "sum"])
        total = LP[0, dy].astype(F32) + XR2[0, dy].astype(F32) + XR2[1, dy].astype(F32)
        if dy:
            RB[dy - 1] = total.astype(BF16)
        else:
            RF[...] = total

    def y_raw():
        y_msg[1, "raw"] = message(RB.at[0, HIGH], YR2.at[0, HIGH], to_y[1])
        y_msg[-1, "raw"] = message(RB.at[2, LOW], YR2.at[1, LOW], to_y[-1])

    def y_first():
        y_msg[1, "far"] = message(RB.at[1, LOW], YR1.at[0], to_y[1])
        y_msg[-1, "far"] = message(RB.at[1, HIGH], YR1.at[1], to_y[-1])

    def y_second():
        arrive(y_msg[1, "far"])
        YS[0] = (RB[0, 0:2].astype(F32) + YR1[0].astype(F32)).astype(BF16)
        y_msg[1, "sum"] = message(YS.at[0], YR2.at[0, LOW], to_y[1])
        arrive(y_msg[-1, "far"])
        YS[1] = (RB[2, 2:4].astype(F32) + YR1[1].astype(F32)).astype(BF16)
        y_msg[-1, "sum"] = message(YS.at[1], YR2.at[1, HIGH], to_y[-1])

    own = {}

    def y_last():
        for way in (1, -1):
            arrive(y_msg[way, "raw"])
            arrive(y_msg[way, "sum"])
        total = (RF[...] + YR2[0].astype(F32) + YR2[1].astype(F32)) * scale
        left, right = total[:, :, 0:128], total[:, :, 128:256]
        SB[...] = jnp.where(c == 0, right, left).astype(BF16)
        own["copy"] = message(SB, SBR, sib)
        wg_out[pl.ds(4 * c, 4)] = jnp.where(c == 0, left, right).astype(BF16)

    def put_back(b, store):
        for n in range(D // CT):
            cols = slice(n * CT, (n + 1) * CT)
            store(cols, nn_dot(PT[b], PGB[b, :, :, cols].reshape(256, CT)))

    d_msg, e_msg = {}, {}

    def for_sibling(dz):
        def store(cols, value):
            DP[dz, :, cols] = value.astype(BF16)

        put_back(slot_of(dz, 1), store)
        d_msg[dz] = message(DP.at[dz], DS.at[dz], sib)

    def for_self(dz):
        arrive(d_msg[dz])

        def store(cols, value):
            EF[dz, :, cols] = value + DS[dz, :, cols].astype(F32)

        put_back(slot_of(dz, 0), store)

    def z_parts(t, way):
        if t == 1:
            return ["A"] if way > 0 else ["B"]
        return ["A", "B"] if way > 0 else ["B", "A"]

    def z_place(t, way):
        return (5 - t) if way > 0 else (NZ - 5 + t) % NZ

    def z_send(t, way, half):
        lane_of = 0 if way > 0 else 1
        value = EF[z_place(t, way), HALF[half], :]
        if t > 1 and half in z_parts(t - 1, way):
            arrive(e_msg[t - 1, way, half])
            value = value + ZR[lane_of, t - 2, HALF[half], :].astype(F32)
        ZS[lane_of, t - 1, HALF[half], :] = value.astype(BF16)
        e_msg[t, way, half] = message(
            ZS.at[lane_of, t - 1, HALF[half]], ZR.at[lane_of, t - 1, HALF[half]], to_z[way]
        )

    clusters(0)
    x_first(0)
    for k in range(4):
        arrive(w_msg[1, k])
    clusters(1)
    x_second(0)
    x_first(1)
    for k in range(4):
        arrive(w_msg[3, k])
    arrive(z_msg[3])
    clusters(3)
    x_second(1)
    x_first(3)
    for k in range(4):
        arrive(w_msg[2, k])
    arrive(z_msg[2])
    clusters(2)
    x_first(2)
    x_second(3)
    for_sibling(4)
    for_sibling(3)
    for_sibling(5)
    for_self(4)
    z_send(1, 1, "A")
    z_send(1, -1, "B")
    for_self(3)
    z_send(2, 1, "B")
    for_self(5)
    z_send(2, -1, "A")
    x_second(2)
    for dz in (2, 6, 1, 7, 0):
        for_sibling(dz)
    z_send(2, 1, "A")
    z_send(2, -1, "B")
    x_last(0)
    x_last(1)
    x_last(3)
    y_raw()
    for_self(2)
    for_self(6)
    x_last(2)
    y_first()
    z_send(3, 1, "A")
    z_send(3, -1, "B")
    z_send(3, 1, "B")
    z_send(3, -1, "A")
    for_self(1)
    for_self(7)
    y_second()
    z_send(4, 1, "A")
    z_send(4, -1, "B")
    z_send(4, 1, "B")
    z_send(4, -1, "A")
    for_self(0)
    y_last()
    arrive(own["copy"])
    wg_out[pl.ds(4 * (1 - c), 4)] = SBR[...]
    for half in ("A", "B"):
        arrive(e_msg[4, 1, half])
        arrive(e_msg[4, -1, half])
        rows = HALF[half]
        df_out[rows, :] = (
            EF[0, rows, :] + ZR[0, 3, rows, :].astype(F32) + ZR[1, 3, rows, :].astype(F32)
        ).astype(BF16)
    for copy in sent:
        copy.wait_send()


MESSAGES = 160


def local(features, shortlist, positives, cluster_sizes, weights):
    pairs_mean = features.shape[0] * lax.axis_size("seq") * shortlist.shape[1] // cluster_sizes.shape[0]
    vmem = pl.BlockSpec(memory_space=pltpu.VMEM)
    anywhere = pl.BlockSpec(memory_space=pl.ANY)

    def kernel(*refs):
        body(1.0 / math.sqrt(pairs_mean), *refs)

    feature_grad, weight_grad = pl.pallas_call(
        kernel,
        out_shape=(
            jax.ShapeDtypeStruct((BLK, D), BF16),
            jax.ShapeDtypeStruct((8, BLK, BLK), BF16),
        ),
        in_specs=[anywhere, vmem, vmem, pl.BlockSpec(memory_space=pltpu.SMEM), anywhere],
        out_specs=(vmem, vmem),
        scratch_shapes=[
            pltpu.VMEM((NB, BLK, D), BF16),
            pltpu.VMEM((NB, 48, BLK), BF16),
            pltpu.VMEM((NY, 4, BLK, D), BF16),
            pltpu.VMEM((NY, 8, BLK), F32),
            pltpu.VMEM((NK, NB, SLOTS, D), BF16),
            pltpu.VMEM((NB, NK, SLOTS, D), BF16),
            pltpu.VMEM((NK, NB, SLOTS, 16), F32),
            pltpu.VMEM((NB, 256, BLK), BF16),
            pltpu.VMEM((NB, BLK, 256), BF16),
            pltpu.VMEM((NX, NY, 4, BLK, CT), BF16),
            pltpu.VMEM((2, NY, 2, BLK, CT), BF16),
            pltpu.VMEM((2, NY, 2, BLK, CT), BF16),
            pltpu.VMEM((2, NY, 4, BLK, CT), BF16),
            pltpu.VMEM((3, 4, BLK, CT), BF16),
            pltpu.VMEM((4, BLK, CT), F32),
            pltpu.VMEM((2, 2, BLK, CT), BF16),
            pltpu.VMEM((2, 2, BLK, CT), BF16),
            pltpu.VMEM((2, 4, BLK, CT), BF16),
            pltpu.VMEM((4, BLK, BLK), BF16),
            pltpu.VMEM((4, BLK, BLK), BF16),
            pltpu.VMEM((NZ, BLK, D), BF16),
            pltpu.VMEM((NZ, BLK, D), BF16),
            pltpu.VMEM((NZ, BLK, D), F32),
            pltpu.VMEM((2, 4, BLK, D), BF16),
            pltpu.VMEM((2, 4, BLK, D), BF16),
            pltpu.SemaphoreType.DMA((MESSAGES,)),
            pltpu.SemaphoreType.DMA((MESSAGES,)),
            pltpu.SemaphoreType.DMA((2,)),
        ],
        compiler_params=pltpu.CompilerParams(
            collective_id=0, has_side_effects=True, vmem_limit_bytes=60 << 20
        ),
        name="ranker",
    )(features, shortlist.T, positives.T, cluster_sizes, weights.reshape(8, BLK, D))
    return feature_grad, weight_grad.reshape(8 * BLK, BLK)


def solution(mesh):
    return jax.shard_map(
        local,
        mesh=mesh,
        in_specs=(
            P(("seq", "clus"), None),
            P(("seq", "clus"), None),
            P(("seq", "clus"), None),
            P("clus"),
            P("clus", None),
        ),
        out_specs=(P(("seq", "clus"), None), P("clus", "seq")),
        check_vma=False,
    )
```

```python
import math

import jax
import jax.numpy as jnp
from jax import lax
from jax.experimental import pallas as pl
from jax.experimental.pallas import tpu as pltpu
from jax.sharding import PartitionSpec as P

MESH = pl.DeviceIdType.MESH
NX, NY, NZ = 4, 4, 8
BLK = 128
SLOTS = 16
NB = 16
NK = 16
D = 1024
CT = 256
F32, BF16 = jnp.float32, jnp.bfloat16


def slot_of(dz, dc):
    hop = min(dz, NZ - dz)
    if hop == 0:
        return dc
    if hop == NZ // 2:
        return NB - 2 + dc
    return 4 * hop - 2 + (0 if dz < NZ // 2 else 1) + 2 * dc


def nt_dot(a, b):
    return lax.dot_general(a, b, (((1,), (1,)), ((), ())), preferred_element_type=F32)


def nn_dot(a, b):
    return jnp.dot(a, b, preferred_element_type=F32)


def body(
    scale, f_in, sl_in, pos_in, sz_in, w_in, df_out, wg_out,
    F, M, W, SZ, X, PGB, TG, PM, PT, LP, RS, R1, R2, RB, RF, SB, SBR,
    DP, DS, EF, ZS, ZR, send_sems, recv_sems, local_sems,
):
    s, q = lax.axis_index("seq"), lax.axis_index("clus")
    x, c, y, z = s // 2, s % 2, q // NZ, q % NZ
    sib = (s + 1 - 2 * c, q)
    to_x = {1: ((s + 2) % 8, q), -1: ((s + 6) % 8, q)}
    to_y = {1: (s, (q + 8) % 32), -1: (s, (q + 24) % 32)}
    to_z = {1: (s, y * 8 + (z + 1) % 8), -1: (s, y * 8 + (z + 7) % 8)}
    partners = [sib, *to_x.values(), *to_y.values(), *to_z.values()]
    sent, arrived = [], set()

    def arrive(copy):
        if id(copy) not in arrived:
            arrived.add(id(copy))
            copy.wait_recv()

    def message(src, dst, device):
        number = len(sent)
        copy = pltpu.make_async_remote_copy(
            src_ref=src, dst_ref=dst, send_sem=send_sems.at[number], recv_sem=recv_sems.at[number],
            device_id=device, device_id_type=MESH,
        )
        copy.start()
        sent.append(copy)
        return copy

    cp_f = pltpu.make_async_copy(f_in, F.at[0], local_sems.at[0])
    cp_w = pltpu.make_async_copy(w_in.at[pl.ds(4 * c, 4)], W.at[0], local_sems.at[1])
    cp_f.start()
    cp_w.start()
    barrier = pltpu.get_barrier_semaphore()
    for device in partners:
        pl.semaphore_signal(barrier, inc=1, device_id=device, device_id_type=MESH)

    short = sl_in[...]
    place_row = lax.broadcasted_iota(jnp.int32, (16, BLK), 0)
    pos_cl = jnp.full((16, BLK), -1.0, F32)
    pos_off = jnp.full((16, BLK), -1.0, F32)
    for j in range(4):
        code = pos_in[j : j + 1, :]
        named = jnp.sum(jnp.where(place_row == (code >> 7), short, 0), axis=0, keepdims=True)
        pos_cl = jnp.where(place_row == j, named.astype(F32), pos_cl)
        pos_off = jnp.where(place_row == j, (code & 127).astype(F32), pos_off)
    M[0, 0:16, :] = short.astype(F32).astype(BF16)
    M[0, 16:32, :] = pos_cl.astype(BF16)
    M[0, 32:48, :] = pos_off.astype(BF16)
    row8 = lax.broadcasted_iota(jnp.int32, (8, BLK), 0)
    sizes = jnp.zeros((8, BLK), F32)
    for k in range(4):
        sizes = jnp.where(row8 == k, sz_in[4 * c + k].astype(F32), sizes)
    SZ[0] = sizes

    pl.semaphore_wait(barrier, len(partners))

    HALF = {"A": pl.ds(0, 64), "B": pl.ds(64, 64)}

    def landing(h, way):
        return h if way < 0 else NZ - h

    f_msg, m_msg, sf_msg, sm_msg = {}, {}, {}, {}

    def halves(h, way):
        if h == 4:
            return ["A"] if way < 0 else ["B"]
        return ["A", "B"] if way < 0 else ["B", "A"]

    def send_half(h, way, half):
        src = slot_of(landing(h - 1, way) % NZ, 0)
        dst = slot_of(landing(h, way), 0)
        f_msg[h, way, half] = message(F.at[src, HALF[half]], F.at[dst, HALF[half]], to_z[way])

    def send_meta(h, way):
        src = slot_of(landing(h - 1, way) % NZ, 0)
        dst = slot_of(landing(h, way), 0)
        m_msg[h, way] = message(M.at[src], M.at[dst], to_z[way])

    def share_half(dz, half):
        sf_msg[dz, half] = message(
            F.at[slot_of(dz, 0), HALF[half]], F.at[slot_of(dz, 1), HALF[half]], sib
        )

    def share_meta(dz):
        sm_msg[dz] = message(M.at[slot_of(dz, 0)], M.at[slot_of(dz, 1)], sib)

    w_msg, z_msg = {}, {}

    for way in (-1, 1):
        send_meta(1, way)
    share_meta(0)
    cp_f.wait()
    for i in range(2):
        for way in (-1, 1):
            send_half(1, way, halves(1, way)[i])
    share_half(0, "A")
    share_half(0, "B")
    z_msg[1] = message(SZ.at[0], SZ.at[1], to_y[-1])
    z_msg[3] = message(SZ.at[0], SZ.at[3], to_y[1])
    cp_w.wait()
    def near_weights(i):
        k = (x + i) % 4
        w_msg[1, i] = message(W.at[0, k], W.at[1, k], to_y[-1])
        w_msg[3, i] = message(W.at[0, k], W.at[3, k], to_y[1])

    near_weights(0)
    near_weights(1)

    def opposite_weights():
        arrive(w_msg[1, 0])
        w_msg["y", -1] = message(W.at[1, x, HALF["A"]], W.at[2, x, HALF["A"]], to_y[-1])
        arrive(w_msg[3, 0])
        w_msg["y", 1] = message(W.at[3, x, HALF["B"]], W.at[2, x, HALF["B"]], to_y[1])
        near_weights(2)
        near_weights(3)

    def spread_weights():
        arrive(w_msg["y", -1])
        arrive(w_msg["y", 1])
        for way in (-1, 1):
            w_msg["x", way] = message(W.at[2, x], W.at[2, x], to_x[way])

    def pass_weights():
        after, before = (x + 1) % 4, (x + 3) % 4
        arrive(w_msg["x", -1])
        w_msg["xx", -1] = message(W.at[2, after, HALF["A"]], W.at[2, after, HALF["A"]], to_x[-1])
        arrive(w_msg["x", 1])
        w_msg["xx", 1] = message(W.at[2, before, HALF["B"]], W.at[2, before, HALF["B"]], to_x[1])

    kk16 = lax.broadcasted_iota(jnp.int32, (16, BLK), 0)
    cid16 = (((((y + (kk16 >> 2)) & 3) * 8 + z) * 8) + 4 * c + (kk16 & 3)).astype(F32)
    kk256 = lax.broadcasted_iota(jnp.int32, (256, 16), 0) >> 4
    cid256 = (((((y + (kk256 >> 2)) & 3) * 8 + z) * 8) + 4 * c + (kk256 & 3)).astype(F32)
    slot_row = lax.broadcasted_iota(jnp.int32, (16, BLK), 0).astype(F32)

    def pick(b):
        names = M[b, 0:16, :].astype(F32)
        member = jnp.zeros((16, BLK), F32)
        for j in range(16):
            member = member + jnp.where(names[j : j + 1, :] == cid16, 1.0, 0.0)
        before = (
            lax.broadcasted_iota(jnp.int32, (BLK, BLK), 0)
            < lax.broadcasted_iota(jnp.int32, (BLK, BLK), 1)
        )
        rank = nn_dot(member.astype(BF16), jnp.where(before, 1.0, 0.0).astype(BF16))
        rank = jnp.where(member > 0.0, rank, -1.0)
        for k in range(NK):
            PM[b, k * 16 : (k + 1) * 16, :] = jnp.where(
                rank[k : k + 1, :] == slot_row, 1.0, 0.0
            ).astype(BF16)
        picks = PM[b]
        PT[b] = jnp.transpose(picks.astype(F32)).astype(BF16)
        named = nt_dot(picks, M[b, 16:32, :])
        offset = nt_dot(picks, M[b, 32:48, :])
        TG[:, b] = jnp.where(named == cid256, offset, -1.0).reshape(16, 16, 16)
        for n in range(D // CT):
            cols = slice(n * CT, (n + 1) * CT)
            X[:, b, :, cols] = nn_dot(picks, F[b, :, cols]).astype(BF16).reshape(16, 16, CT)

    def pick_range(first, count):
        lax.fori_loop(0, count, lambda i, _: (pick(first + i), 0)[1], 0, unroll=count)

    def await_shared(dz):
        arrive(sm_msg[dz])
        arrive(sf_msg[dz, "A"])
        arrive(sf_msg[dz, "B"])

    pick_range(0, 1)
    for h in range(1, 5):
        for i in range(2 if h < 4 else 1):
            for way in (-1, 1):
                half = halves(h, way)[i]
                arrive(f_msg[h, way, half])
                if h < 4 and half in halves(h + 1, way):
                    send_half(h + 1, way, half)
            for way in (-1, 1):
                half = halves(h, way)[i]
                share_half(landing(h, way), half)
        for way in (-1, 1):
            if h < 4 or way < 0:
                arrive(m_msg[h, way])
                if h < 3 or (h == 3 and way < 0):
                    send_meta(h + 1, way)
                share_meta(landing(h, way))
        if h == 1:
            opposite_weights()
            arrive(z_msg[1])
            z_msg[2] = message(SZ.at[1], SZ.at[2], to_y[-1])
        if h == 3:
            spread_weights()
        if h < 4:
            pick_range(4 * h - 2, 2)
        else:
            pick_range(14, 1)
        if h == 1:
            await_shared(0)
            pick_range(1, 1)
        else:
            await_shared(h - 1)
            await_shared(NZ - h + 1)
            pick_range(4 * (h - 1), 2)
    await_shared(4)
    pick_range(15, 1)

    lane = lax.broadcasted_iota(jnp.int32, (256, BLK), 1).astype(F32)

    def cluster(dy, k):
        kk = 4 * dy + k
        weights = W[dy, k]
        logits = nt_dot(X[kk].reshape(256, D), weights)
        target = TG[kk].reshape(256, 16)
        positive = target[:, 0:1] == lane
        for j in range(1, 4):
            positive = positive | (target[:, j : j + 1] == lane)
        sign = jnp.where(positive, 1.0, -1.0)
        live = lane < SZ[dy, pl.ds(k, 1), :]
        slope = jnp.where(live, -2.0 * sign * jnp.maximum(1.0 - sign * logits, 0.0), 0.0)
        turned = jnp.transpose(slope).astype(BF16)
        slope = slope.astype(BF16)
        for dx in range(NX):
            cols = pl.ds(pl.multiple_of(CT * ((x + dx) % NX), CT), CT)
            part = nn_dot(turned, X[kk, :, :, cols].reshape(256, CT))
            LP[dx, dy, k] = part.astype(BF16)
        for n in range(D // CT):
            cols = slice(n * CT, (n + 1) * CT)
            PGB[:, kk, :, cols] = nn_dot(slope, W[dy, k, :, cols]).astype(BF16).reshape(16, 16, CT)

    def clusters(dy):
        lax.fori_loop(0, 4, lambda k, _: (cluster(dy, k), 0)[1], 0, unroll=4)

    class Ring:
        def __init__(self, number, to, part, own):
            self.number, self.to, self.part, self.own = number, to, part, own
            self.msg = {}

        def far(self):
            n = self.number
            self.msg["far", 0] = message(self.part(2, 0), R1.at[n, 0], self.to[1])
            self.msg["far", 1] = message(self.part(2, 1), R1.at[n, 1], self.to[-1])

        def raw(self):
            n = self.number
            self.msg["raw", 0] = message(self.part(1, 1), R2.at[n, 0, 1], self.to[1])
            self.msg["raw", 1] = message(self.part(3, 0), R2.at[n, 1, 0], self.to[-1])

        def second(self):
            n = self.number
            for i, rel, way in ((0, 1, 1), (1, 3, -1)):
                arrive(self.msg["far", i])
                RS[n, i] = (self.part(rel, i)[...].astype(F32) + R1[n, i].astype(F32)).astype(BF16)
                self.msg["sum", i] = message(RS.at[n, i], R2.at[n, i, i], self.to[way])

        def last(self, half):
            n = self.number
            arrive(self.msg["raw" if half else "sum", 0])
            arrive(self.msg["sum" if half else "raw", 1])
            return self.own(half) + R2[n, 0, half].astype(F32) + R2[n, 1, half].astype(F32)

    def own_part(dx, dy, k):
        return LP[dx, dy, k].astype(F32)

    low_x = [
        Ring(dy, to_x, lambda dx, h, dy=dy: LP.at[dx, dy, h], lambda h, dy=dy: own_part(0, dy, h))
        for dy in range(NY)
    ]
    low_y = Ring(4, to_y, lambda dy, h: RB.at[0, dy, h], lambda h: RF[0, h])
    high_y = [
        Ring(5 + dx, to_y, lambda dy, h, dx=dx: LP.at[dx, dy, 2 + h], lambda h, dx=dx: own_part(dx, 0, 2 + h))
        for dx in range(NX)
    ]
    high_x = Ring(9, to_x, lambda dx, h: RB.at[1, dx, h], lambda h: RF[1, h])

    def settle(ring, group, place):
        for half in range(2):
            total = ring.last(half)
            if place:
                RB[group, place, half] = total.astype(BF16)
            else:
                RF[group, half] = total

    own = {}

    def finish(ring, group):
        for half in range(2):
            k = 2 * group + half
            total = ring.last(half) * scale
            left, right = total[:, 0:128], total[:, 128:256]
            SB[k] = jnp.where(c == 0, right, left).astype(BF16)
            wg_out[4 * c + k] = jnp.where(c == 0, left, right).astype(BF16)
        own[group] = message(SB.at[pl.ds(2 * group, 2)], SBR.at[pl.ds(2 * group, 2)], sib)

    def put_back(b, store):
        for n in range(D // CT):
            cols = slice(n * CT, (n + 1) * CT)
            store(cols, nn_dot(PT[b], PGB[b, :, :, cols].reshape(256, CT)))

    d_msg, e_msg = {}, {}

    def for_sibling(dz):
        def store(cols, value):
            DP[dz, :, cols] = value.astype(BF16)

        put_back(slot_of(dz, 1), store)
        d_msg[dz] = message(DP.at[dz], DS.at[dz], sib)

    def for_self(dz):
        arrive(d_msg[dz])

        def store(cols, value):
            EF[dz, :, cols] = value + DS[dz, :, cols].astype(F32)

        put_back(slot_of(dz, 0), store)

    def z_parts(t, way):
        if t == 1:
            return ["A"] if way > 0 else ["B"]
        return ["A", "B"] if way > 0 else ["B", "A"]

    def z_place(t, way):
        return (5 - t) if way > 0 else (NZ - 5 + t) % NZ

    def z_send(t, way, half):
        lane_of = 0 if way > 0 else 1
        value = EF[z_place(t, way), HALF[half], :]
        if t > 1 and half in z_parts(t - 1, way):
            arrive(e_msg[t - 1, way, half])
            value = value + ZR[lane_of, t - 2, HALF[half], :].astype(F32)
        ZS[lane_of, t - 1, HALF[half], :] = value.astype(BF16)
        e_msg[t, way, half] = message(
            ZS.at[lane_of, t - 1, HALF[half]], ZR.at[lane_of, t - 1, HALF[half]], to_z[way]
        )

    pass_weights()
    clusters(0)
    low_x[0].far()
    low_x[0].raw()
    for i in range(4):
        arrive(w_msg[1, i])
    clusters(1)
    low_x[1].far()
    low_x[1].raw()
    for i in range(4):
        arrive(w_msg[3, i])
    arrive(z_msg[3])
    clusters(3)
    low_x[3].far()
    low_x[3].raw()
    low_x[0].second()
    arrive(w_msg["xx", -1])
    arrive(w_msg["xx", 1])
    arrive(z_msg[2])
    clusters(2)
    for dz in (4, 3, 5):
        for_sibling(dz)
    low_x[2].far()
    for dx in (2, 1, 3, 0):
        high_y[dx].far()
    low_x[2].raw()
    for dx in (2, 1, 3, 0):
        high_y[dx].raw()
    low_x[1].second()
    for_self(4)
    z_send(1, 1, "A")
    z_send(1, -1, "B")
    for_sibling(2)
    for_sibling(6)
    for_self(3)
    z_send(2, 1, "B")
    for_self(5)
    z_send(2, -1, "A")
    for dz in (1, 7, 0):
        for_sibling(dz)
    low_x[3].second()
    low_x[2].second()
    for_self(2)
    for_self(6)
    for_self(1)
    for_self(7)
    for_self(0)
    high_y[2].second()
    z_send(2, 1, "A")
    z_send(2, -1, "B")
    for dx in (1, 3, 0):
        high_y[dx].second()
    for dy in (0, 1, 3):
        settle(low_x[dy], 0, dy)
    low_y.raw()
    z_send(3, 1, "A")
    z_send(3, -1, "B")
    settle(low_x[2], 0, 2)
    low_y.far()
    z_send(3, 1, "B")
    z_send(3, -1, "A")
    settle(high_y[2], 1, 2)
    high_x.far()
    settle(high_y[1], 1, 1)
    settle(high_y[3], 1, 3)
    high_x.raw()
    low_y.second()
    z_send(4, 1, "A")
    z_send(4, -1, "B")
    high_x.second()
    z_send(4, 1, "B")
    z_send(4, -1, "A")
    settle(high_y[0], 1, 0)
    finish(low_y, 0)
    finish(high_x, 1)
    for half in ("A", "B"):
        arrive(e_msg[4, 1, half])
        arrive(e_msg[4, -1, half])
        rows = HALF[half]
        df_out[rows, :] = (
            EF[0, rows, :] + ZR[0, 3, rows, :].astype(F32) + ZR[1, 3, rows, :].astype(F32)
        ).astype(BF16)
    for group in range(2):
        arrive(own[group])
    wg_out[pl.ds(4 * (1 - c), 4)] = SBR[...]
    for copy in sent:
        copy.wait_send()


MESSAGES = 160


def local(features, shortlist, positives, cluster_sizes, weights):
    pairs_mean = features.shape[0] * lax.axis_size("seq") * shortlist.shape[1] // cluster_sizes.shape[0]
    vmem = pl.BlockSpec(memory_space=pltpu.VMEM)
    anywhere = pl.BlockSpec(memory_space=pl.ANY)

    def kernel(*refs):
        body(1.0 / math.sqrt(pairs_mean), *refs)

    feature_grad, weight_grad = pl.pallas_call(
        kernel,
        out_shape=(
            jax.ShapeDtypeStruct((BLK, D), BF16),
            jax.ShapeDtypeStruct((8, BLK, BLK), BF16),
        ),
        in_specs=[anywhere, vmem, vmem, pl.BlockSpec(memory_space=pltpu.SMEM), anywhere],
        out_specs=(vmem, vmem),
        scratch_shapes=[
            pltpu.VMEM((NB, BLK, D), BF16),
            pltpu.VMEM((NB, 48, BLK), BF16),
            pltpu.VMEM((NY, 4, BLK, D), BF16),
            pltpu.VMEM((NY, 8, BLK), F32),
            pltpu.VMEM((NK, NB, SLOTS, D), BF16),
            pltpu.VMEM((NB, NK, SLOTS, D), BF16),
            pltpu.VMEM((NK, NB, SLOTS, 16), F32),
            pltpu.VMEM((NB, 256, BLK), BF16),
            pltpu.VMEM((NB, BLK, 256), BF16),
            pltpu.VMEM((NX, NY, 4, BLK, CT), BF16),
            pltpu.VMEM((10, 2, BLK, CT), BF16),
            pltpu.VMEM((10, 2, BLK, CT), BF16),
            pltpu.VMEM((10, 2, 2, BLK, CT), BF16),
            pltpu.VMEM((2, 4, 2, BLK, CT), BF16),
            pltpu.VMEM((2, 2, BLK, CT), F32),
            pltpu.VMEM((4, BLK, BLK), BF16),
            pltpu.VMEM((4, BLK, BLK), BF16),
            pltpu.VMEM((NZ, BLK, D), BF16),
            pltpu.VMEM((NZ, BLK, D), BF16),
            pltpu.VMEM((NZ, BLK, D), F32),
            pltpu.VMEM((2, 4, BLK, D), BF16),
            pltpu.VMEM((2, 4, BLK, D), BF16),
            pltpu.SemaphoreType.DMA((MESSAGES,)),
            pltpu.SemaphoreType.DMA((MESSAGES,)),
            pltpu.SemaphoreType.DMA((2,)),
        ],
        compiler_params=pltpu.CompilerParams(
            collective_id=0, has_side_effects=True, vmem_limit_bytes=60 << 20
        ),
        name="ranker",
    )(features, shortlist.T, positives.T, cluster_sizes, weights.reshape(8, BLK, D))
    return feature_grad, weight_grad.reshape(8 * BLK, BLK)


def solution(mesh):
    return jax.shard_map(
        local,
        mesh=mesh,
        in_specs=(
            P(("seq", "clus"), None),
            P(("seq", "clus"), None),
            P(("seq", "clus"), None),
            P("clus"),
            P("clus", None),
        ),
        out_specs=(P(("seq", "clus"), None), P("clus", "seq")),
        check_vma=False,
    )
```

```python
import math

import jax
import jax.numpy as jnp
from jax import lax
from jax.experimental import pallas as pl
from jax.experimental.pallas import tpu as pltpu
from jax.sharding import PartitionSpec as P

MESH = pl.DeviceIdType.MESH
NX, NY, NZ = 4, 4, 8
BLK = 128
SLOTS = 16
NB = 16
NK = 16
D = 1024
CT = 256
F32, BF16 = jnp.float32, jnp.bfloat16


ORDER = (
    "p0", "q0", "m1", "f10", "f11", "wo", "wn", "f12", "f13", "p1", "wm", "m2", "q1", "f20", "ws", "f21", "f22",
    "f23", "p2", "m3", "q2", "f30", "n0", "f31", "e0", "wp", "e1", "f32", "e3", "f33", "p3", "m4", "q3", "f40",
    "e2", "f41", "p4", "n2", "q4", "r", "b2", "b3", "b1", "ds3", "ds4", "ds5", "ds0", "ds6", "lf2", "ds1", "ds7",
    "lr6", "ds2", "lf7", "b0", "lr2", "lf6", "de3", "lr7", "lr8", "lf1", "lr5", "lf8", "lf0", "lr3", "de4", "z11",
    "z10", "lr0", "de5", "z22", "z23", "lr1", "de0", "lf3", "lf5", "l22", "de6", "de1", "de7", "l27", "de2",
    "z21", "l21", "l26", "z20", "l20", "z32", "z33", "z31", "l28", "z30", "l23", "l25", "z42", "l32", "lf4",
    "l37", "lf9", "z43", "l31", "l36", "z41", "l30", "l38", "lr9", "z40", "l33", "lr4", "l35", "l29", "l24",
    "zf1", "zf2", "zf0", "zf3", "l39", "l34", "end",
)


def slot_of(dz, dc):
    hop = min(dz, NZ - dz)
    if hop == 0:
        return dc
    if hop == NZ // 2:
        return NB - 2 + dc
    return 4 * hop - 2 + (0 if dz < NZ // 2 else 1) + 2 * dc


def nt_dot(a, b):
    return lax.dot_general(a, b, (((1,), (1,)), ((), ())), preferred_element_type=F32)


def nn_dot(a, b):
    return jnp.dot(a, b, preferred_element_type=F32)


def body(
    scale, f_in, sl_in, pos_in, sz_in, w_in, df_out, wg_out,
    F, M, W, SZ, X, PGB, TG, PM, PT, SL, LP, RS, R1, R2, RB, RF, SB, SBR,
    DP, DS, EF, ZS, ZR, send_sems, recv_sems, local_sems,
):
    s, q = lax.axis_index("seq"), lax.axis_index("clus")
    x, c, y, z = s // 2, s % 2, q // NZ, q % NZ
    sib = (s + 1 - 2 * c, q)
    to_x = {1: ((s + 2) % 8, q), -1: ((s + 6) % 8, q)}
    to_y = {1: (s, (q + 8) % 32), -1: (s, (q + 24) % 32)}
    to_z = {1: (s, y * 8 + (z + 1) % 8), -1: (s, y * 8 + (z + 7) % 8)}
    partners = [sib, *to_x.values(), *to_y.values(), *to_z.values()]
    sent, arrived = [], set()

    def arrive(copy):
        if id(copy) not in arrived:
            arrived.add(id(copy))
            copy.wait_recv()

    def message(src, dst, device):
        number = len(sent)
        copy = pltpu.make_async_remote_copy(
            src_ref=src, dst_ref=dst, send_sem=send_sems.at[number], recv_sem=recv_sems.at[number],
            device_id=device, device_id_type=MESH,
        )
        copy.start()
        sent.append(copy)
        return copy

    cp_f = pltpu.make_async_copy(f_in, F.at[0], local_sems.at[0])
    cp_w = pltpu.make_async_copy(w_in.at[pl.ds(4 * c, 4)], W.at[0], local_sems.at[1])
    cp_f.start()
    cp_w.start()
    barrier = pltpu.get_barrier_semaphore()
    for device in partners:
        pl.semaphore_signal(barrier, inc=1, device_id=device, device_id_type=MESH)

    short = sl_in[...]
    place_row = lax.broadcasted_iota(jnp.int32, (16, BLK), 0)
    pos_cl = jnp.full((16, BLK), -1.0, F32)
    pos_off = jnp.full((16, BLK), -1.0, F32)
    for j in range(4):
        code = pos_in[j : j + 1, :]
        named = jnp.sum(jnp.where(place_row == (code >> 7), short, 0), axis=0, keepdims=True)
        pos_cl = jnp.where(place_row == j, named.astype(F32), pos_cl)
        pos_off = jnp.where(place_row == j, (code & 127).astype(F32), pos_off)
    M[0, 0:16, :] = short.astype(F32).astype(BF16)
    M[0, 16:32, :] = pos_cl.astype(BF16)
    M[0, 32:48, :] = pos_off.astype(BF16)
    row8 = lax.broadcasted_iota(jnp.int32, (8, BLK), 0)
    sizes = jnp.zeros((8, BLK), F32)
    for k in range(4):
        sizes = jnp.where(row8 == k, sz_in[4 * c + k].astype(F32), sizes)
    SZ[0] = sizes

    pl.semaphore_wait(barrier, len(partners))

    HALF = {"A": pl.ds(0, 64), "B": pl.ds(64, 64)}
    PIECE = [pl.ds(32 * p, 32) for p in range(4)]
    tasks = {}

    def landing(h, way):
        return h if way < 0 else NZ - h

    f_msg, m_msg, sf_msg, sm_msg = {}, {}, {}, {}

    def pieces(h, way):
        order = [0, 1, 2, 3] if way < 0 else [3, 2, 1, 0]
        return order[:2] if h == 4 else order

    def send_piece(h, way, p):
        src = slot_of(landing(h - 1, way) % NZ, 0)
        dst = slot_of(landing(h, way), 0)
        f_msg[h, way, p] = message(F.at[src, PIECE[p]], F.at[dst, PIECE[p]], to_z[way])

    def send_meta(h, way):
        src = slot_of(landing(h - 1, way) % NZ, 0)
        dst = slot_of(landing(h, way), 0)
        m_msg[h, way] = message(M.at[src], M.at[dst], to_z[way])

    def share_piece(dz, p):
        sf_msg[dz, p] = message(F.at[slot_of(dz, 0), PIECE[p]], F.at[slot_of(dz, 1), PIECE[p]], sib)

    def share_meta(dz):
        sm_msg[dz] = message(M.at[slot_of(dz, 0)], M.at[slot_of(dz, 1)], sib)

    def feature_step(h, i):
        for way in (-1, 1):
            p = pieces(h, way)[i]
            arrive(f_msg[h, way, p])
            if h < 4 and p in pieces(h + 1, way):
                send_piece(h + 1, way, p)
        for way in (-1, 1):
            share_piece(landing(h, way), pieces(h, way)[i])

    def meta_step(h):
        for way in (-1, 1):
            if h < 4 or way < 0:
                arrive(m_msg[h, way])
                if h < 3 or (h == 3 and way < 0):
                    send_meta(h + 1, way)
                share_meta(landing(h, way))

    w_msg, z_msg = {}, {}

    def near_weights(i, place, way):
        k = (x + i) % 4
        w_msg[place, i] = message(W.at[0, k], W.at[place, k], to_y[way])

    def opposite_weights():
        arrive(w_msg[1, "A"])
        w_msg["y", "A"] = message(W.at[1, x, HALF["A"]], W.at[2, x, HALF["A"]], to_y[-1])
        arrive(w_msg[3, "B"])
        w_msg["y", "B"] = message(W.at[3, x, HALF["B"]], W.at[2, x, HALF["B"]], to_y[1])
        near_weights(1, 1, -1)
        near_weights(2, 3, 1)
        near_weights(2, 1, -1)
        near_weights(3, 3, 1)
        arrive(z_msg[1])
        z_msg[2] = message(SZ.at[1], SZ.at[2], to_y[-1])

    def spread_weights():
        for first, way in (("A", -1), ("B", 1)):
            arrive(w_msg["y", first])
            w_msg["x", way, first] = message(W.at[2, x, HALF[first]], W.at[2, x, HALF[first]], to_x[way])
        for second, way in (("B", -1), ("A", 1)):
            w_msg["x", way, second] = message(W.at[2, x, HALF[second]], W.at[2, x, HALF[second]], to_x[way])

    def pass_weights():
        for half, way, k in (("A", -1, (x + 1) % 4), ("B", 1, (x + 3) % 4)):
            arrive(w_msg["x", way, half])
            w_msg["xx", half] = message(W.at[2, k, HALF[half]], W.at[2, k, HALF[half]], to_x[way])

    def await_opposite():
        for half in ("A", "B"):
            arrive(w_msg["y", half])
            arrive(w_msg["x", -1, half])
            arrive(w_msg["x", 1, half])
            arrive(w_msg["xx", half])
        arrive(z_msg[2])

    def share_near(first):
        for place, way in ((1, 1), (3, -1)):
            half = ("A" if place == 1 else "B") if first else ("B" if place == 1 else "A")
            arrive(w_msg[place, half])
            w_msg["n", place, half] = message(
                W.at[place, x, HALF[half]], W.at[place, x, HALF[half]], to_x[way]
            )

    def await_near(i):
        if i == 0:
            for place in (1, 3):
                arrive(w_msg[place, "A"])
                arrive(w_msg[place, "B"])
            arrive(z_msg[1])
            arrive(z_msg[3])
        elif i == 3:
            for place in (1, 3):
                arrive(w_msg["n", place, "A"])
                arrive(w_msg["n", place, "B"])
        else:
            arrive(w_msg[1, i])
            arrive(w_msg[3, i + 1])

    for way in (-1, 1):
        send_meta(1, way)
    share_meta(0)
    cp_f.wait()
    for i in range(4):
        for way in (-1, 1):
            send_piece(1, way, pieces(1, way)[i])
    sf_msg[0] = message(F.at[slot_of(0, 0)], F.at[slot_of(0, 1)], sib)
    z_msg[1] = message(SZ.at[0], SZ.at[1], to_y[-1])
    z_msg[3] = message(SZ.at[0], SZ.at[3], to_y[1])
    cp_w.wait()
    for place, way, order in ((1, -1, "AB"), (3, 1, "BA")):
        for half in order:
            w_msg[place, half] = message(W.at[0, x, HALF[half]], W.at[place, x, HALF[half]], to_y[way])

    kk16 = lax.broadcasted_iota(jnp.int32, (16, BLK), 0)
    cid16 = (((((y + (kk16 >> 2)) & 3) * 8 + z) * 8) + 4 * c + (kk16 & 3)).astype(F32)
    kk256 = lax.broadcasted_iota(jnp.int32, (256, 16), 0) >> 4
    cid256 = (((((y + (kk256 >> 2)) & 3) * 8 + z) * 8) + 4 * c + (kk256 & 3)).astype(F32)
    slot_row = lax.broadcasted_iota(jnp.int32, (16, BLK), 0).astype(F32)

    def pick(b):
        names = M[b, 0:16, :].astype(F32)
        member = jnp.zeros((16, BLK), F32)
        for j in range(16):
            member = member + jnp.where(names[j : j + 1, :] == cid16, 1.0, 0.0)
        before = (
            lax.broadcasted_iota(jnp.int32, (BLK, BLK), 0)
            < lax.broadcasted_iota(jnp.int32, (BLK, BLK), 1)
        )
        rank = nn_dot(member.astype(BF16), jnp.where(before, 1.0, 0.0).astype(BF16))
        rank = jnp.where(member > 0.0, rank, -1.0)
        for k in range(NK):
            PM[b, k * 16 : (k + 1) * 16, :] = jnp.where(
                rank[k : k + 1, :] == slot_row, 1.0, 0.0
            ).astype(BF16)
        picks = PM[b]
        PT[b] = jnp.transpose(picks.astype(F32)).astype(BF16)
        named = nt_dot(picks, M[b, 16:32, :])
        offset = nt_dot(picks, M[b, 32:48, :])
        TG[:, b] = jnp.where(named == cid256, offset, -1.0).reshape(16, 16, 16)
        for n in range(D // CT):
            cols = slice(n * CT, (n + 1) * CT)
            X[:, b, :, cols] = nn_dot(picks, F[b, :, cols]).astype(BF16).reshape(16, 16, CT)

    def pick_range(first, count):
        lax.fori_loop(0, count, lambda i, _: (pick(first + i), 0)[1], 0, unroll=count)

    def await_shared(dz):
        arrive(sm_msg[dz])
        if dz:
            for p in range(4):
                arrive(sf_msg[dz, p])
        else:
            arrive(sf_msg[0])

    def pick_shared(h):
        for dz in {h, (NZ - h) % NZ}:
            await_shared(dz)
        if h == 0:
            pick_range(1, 1)
        elif h == 4:
            pick_range(15, 1)
        else:
            pick_range(4 * h, 2)

    def pick_own(h):
        if h == 0:
            pick_range(0, 1)
        elif h == 4:
            pick_range(14, 1)
        else:
            pick_range(4 * h - 2, 2)

    for h in range(5):
        tasks[f"p{h}"] = lambda h=h: pick_own(h)
        tasks[f"q{h}"] = lambda h=h: pick_shared(h)
    for h in range(1, 5):
        tasks[f"m{h}"] = lambda h=h: meta_step(h)
        for i in range(len(pieces(h, 1))):
            tasks[f"f{h}{i}"] = lambda h=h, i=i: feature_step(h, i)
    tasks["wo"], tasks["ws"], tasks["wp"] = opposite_weights, spread_weights, pass_weights
    tasks["wn"], tasks["wm"] = lambda: share_near(True), lambda: share_near(False)

    NEAR, FAR = (0, 10), (10, 16)

    def cluster(dy, k, blocks):
        kk = 4 * dy + k
        first, last = blocks
        rows = (last - first) * SLOTS
        lane = lax.broadcasted_iota(jnp.int32, (rows, BLK), 1).astype(F32)
        logits = nt_dot(X[kk, first:last].reshape(rows, D), W[dy, k])
        target = TG[kk, first:last].reshape(rows, 16)
        positive = target[:, 0:1] == lane
        for j in range(1, 4):
            positive = positive | (target[:, j : j + 1] == lane)
        sign = jnp.where(positive, 1.0, -1.0)
        live = lane < SZ[dy, pl.ds(k, 1), :]
        slope = jnp.where(live, -2.0 * sign * jnp.maximum(1.0 - sign * logits, 0.0), 0.0)
        slope = slope.astype(BF16)
        SL[kk, first * SLOTS : last * SLOTS, :] = slope
        for n in range(D // CT):
            cols = slice(n * CT, (n + 1) * CT)
            grads = nn_dot(slope, W[dy, k, :, cols]).astype(BF16)
            PGB[first:last, kk, :, cols] = grads.reshape(last - first, SLOTS, CT)

    def label_part(dy, k):
        kk = 4 * dy + k
        turned = jnp.transpose(SL[kk].astype(F32)).astype(BF16)
        for dx in range(NX):
            cols = pl.ds(pl.multiple_of(CT * ((x + dx) % NX), CT), CT)
            part = nn_dot(turned, X[kk, :, :, cols].reshape(256, CT))
            LP[dx, dy, k] = part.astype(BF16)

    def clusters(pairs, blocks):
        for dy, k in pairs:
            cluster(dy, k, blocks)

    def label_parts(dy):
        for k in range(4):
            label_part(dy, k)

    def opposite_clusters():
        await_opposite()
        clusters([(2, k) for k in range(4)], NEAR)

    def near_clusters(i):
        await_near(i)
        places = {0: (0, 0), 1: (1, 2), 2: (2, 3), 3: (3, 1)}[i]
        clusters([(1, (x + places[0]) % 4), (3, (x + places[1]) % 4)], NEAR)

    def far_clusters():
        def one(dy, carry):
            clusters([(dy, k) for k in range(4)], FAR)
            return carry

        lax.fori_loop(0, NY, one, 0)

    tasks["n0"] = lambda: clusters([(0, k) for k in range(4)], NEAR)
    tasks["n2"] = opposite_clusters
    tasks["r"] = far_clusters
    for i in range(4):
        tasks[f"e{i}"] = lambda i=i: near_clusters(i)
        tasks[f"b{i}"] = lambda i=i: label_parts(i)

    class Ring:
        def __init__(self, number, to, part, own):
            self.number, self.to, self.part, self.own = number, to, part, own
            self.msg = {}

        def far(self):
            n = self.number
            self.msg["far", 0] = message(self.part(2, 0), R1.at[n, 0], self.to[1])
            self.msg["far", 1] = message(self.part(2, 1), R1.at[n, 1], self.to[-1])

        def raw(self):
            n = self.number
            self.msg["raw", 0] = message(self.part(1, 1), R2.at[n, 0, 1], self.to[1])
            self.msg["raw", 1] = message(self.part(3, 0), R2.at[n, 1, 0], self.to[-1])

        def second(self):
            n = self.number
            for i, rel, way in ((0, 1, 1), (1, 3, -1)):
                arrive(self.msg["far", i])
                RS[n, i] = (self.part(rel, i)[...].astype(F32) + R1[n, i].astype(F32)).astype(BF16)
                self.msg["sum", i] = message(RS.at[n, i], R2.at[n, i, i], self.to[way])

        def last(self, half):
            n = self.number
            arrive(self.msg["raw" if half else "sum", 0])
            arrive(self.msg["sum" if half else "raw", 1])
            return self.own(half) + R2[n, 0, half].astype(F32) + R2[n, 1, half].astype(F32)

    def own_part(dx, dy, k):
        return LP[dx, dy, k].astype(F32)

    low_x = [
        Ring(dy, to_x, lambda dx, h, dy=dy: LP.at[dx, dy, h], lambda h, dy=dy: own_part(0, dy, h))
        for dy in range(NY)
    ]
    low_y = Ring(4, to_y, lambda dy, h: RB.at[0, dy, h], lambda h: RF[0, h])
    high_y = [
        Ring(5 + dx, to_y, lambda dy, h, dx=dx: LP.at[dx, dy, 2 + h], lambda h, dx=dx: own_part(dx, 0, 2 + h))
        for dx in range(NX)
    ]
    high_x = Ring(9, to_x, lambda dx, h: RB.at[1, dx, h], lambda h: RF[1, h])

    def settle(ring, group, place):
        for half in range(2):
            total = ring.last(half)
            if place:
                RB[group, place, half] = total.astype(BF16)
            else:
                RF[group, half] = total

    own = {}

    def finish(ring, group):
        for half in range(2):
            k = 2 * group + half
            total = ring.last(half) * scale
            left, right = total[:, 0:128], total[:, 128:256]
            SB[k] = jnp.where(c == 0, right, left).astype(BF16)
            wg_out[4 * c + k] = jnp.where(c == 0, left, right).astype(BF16)
        own[group] = message(SB.at[pl.ds(2 * group, 2)], SBR.at[pl.ds(2 * group, 2)], sib)

    def put_back(b, store):
        for n in range(D // CT):
            cols = slice(n * CT, (n + 1) * CT)
            store(cols, nn_dot(PT[b], PGB[b, :, :, cols].reshape(256, CT)))

    d_msg, e_msg = {}, {}

    def for_sibling(dz):
        def store(cols, value):
            DP[dz, :, cols] = value.astype(BF16)

        put_back(slot_of(dz, 1), store)
        d_msg[dz] = message(DP.at[dz], DS.at[dz], sib)

    def for_self(dz):
        arrive(d_msg[dz])

        def store(cols, value):
            EF[dz, :, cols] = value + DS[dz, :, cols].astype(F32)

        put_back(slot_of(dz, 0), store)

    def z_place(t, way):
        return (5 - t) if way > 0 else (NZ - 5 + t) % NZ

    def z_send(t, way, p):
        lane_of = 0 if way > 0 else 1
        value = EF[z_place(t, way), PIECE[p], :]
        if (t - 1, way, p) in e_msg:
            arrive(e_msg[t - 1, way, p])
            value = value + ZR[lane_of, t - 2, PIECE[p], :].astype(F32)
        ZS[lane_of, t - 1, PIECE[p], :] = value.astype(BF16)
        e_msg[t, way, p] = message(
            ZS.at[lane_of, t - 1, PIECE[p]], ZR.at[lane_of, t - 1, PIECE[p]], to_z[way]
        )

    def z_step(t, p):
        z_send(t, 1, p)
        z_send(t, -1, 3 - p)

    def z_final(p):
        arrive(e_msg[4, 1, p])
        arrive(e_msg[4, -1, p])
        rows = PIECE[p]
        df_out[rows, :] = (
            EF[0, rows, :] + ZR[0, 3, rows, :].astype(F32) + ZR[1, 3, rows, :].astype(F32)
        ).astype(BF16)

    def end():
        for group in range(2):
            arrive(own[group])
        wg_out[pl.ds(4 * (1 - c), 4)] = SBR[...]

    for dz in range(NZ):
        tasks[f"ds{dz}"] = lambda dz=dz: for_sibling(dz)
        tasks[f"de{dz}"] = lambda dz=dz: for_self(dz)
    for p in range(4):
        for t in range(1 if p < 2 else 2, 5):
            tasks[f"z{t}{p}"] = lambda t=t, p=p: z_step(t, p)
        tasks[f"zf{p}"] = lambda p=p: z_final(p)
    for n, ring in enumerate((*low_x, low_y, *high_y, high_x)):
        tasks[f"lf{n}"], tasks[f"lr{n}"], tasks[f"l2{n}"] = ring.far, ring.raw, ring.second
    for i in range(4):
        tasks[f"l3{i}"] = lambda i=i: settle(low_x[i], 0, i)
        tasks[f"l3{5 + i}"] = lambda i=i: settle(high_y[i], 1, i)
    tasks["l34"] = lambda: finish(low_y, 0)
    tasks["l39"] = lambda: finish(high_x, 1)
    tasks["end"] = end

    for name in ORDER:
        tasks.pop(name)()
    assert not tasks
    for copy in sent:
        copy.wait_send()


MESSAGES = 220


def local(features, shortlist, positives, cluster_sizes, weights):
    pairs_mean = features.shape[0] * lax.axis_size("seq") * shortlist.shape[1] // cluster_sizes.shape[0]
    vmem = pl.BlockSpec(memory_space=pltpu.VMEM)
    anywhere = pl.BlockSpec(memory_space=pl.ANY)

    def kernel(*refs):
        body(1.0 / math.sqrt(pairs_mean), *refs)

    feature_grad, weight_grad = pl.pallas_call(
        kernel,
        out_shape=(
            jax.ShapeDtypeStruct((BLK, D), BF16),
            jax.ShapeDtypeStruct((8, BLK, BLK), BF16),
        ),
        in_specs=[anywhere, vmem, vmem, pl.BlockSpec(memory_space=pltpu.SMEM), anywhere],
        out_specs=(vmem, vmem),
        scratch_shapes=[
            pltpu.VMEM((NB, BLK, D), BF16),
            pltpu.VMEM((NB, 48, BLK), BF16),
            pltpu.VMEM((NY, 4, BLK, D), BF16),
            pltpu.VMEM((NY, 8, BLK), F32),
            pltpu.VMEM((NK, NB, SLOTS, D), BF16),
            pltpu.VMEM((NB, NK, SLOTS, D), BF16),
            pltpu.VMEM((NK, NB, SLOTS, 16), F32),
            pltpu.VMEM((NB, 256, BLK), BF16),
            pltpu.VMEM((NB, BLK, 256), BF16),
            pltpu.VMEM((NK, 256, BLK), BF16),
            pltpu.VMEM((NX, NY, 4, BLK, CT), BF16),
            pltpu.VMEM((10, 2, BLK, CT), BF16),
            pltpu.VMEM((10, 2, BLK, CT), BF16),
            pltpu.VMEM((10, 2, 2, BLK, CT), BF16),
            pltpu.VMEM((2, 4, 2, BLK, CT), BF16),
            pltpu.VMEM((2, 2, BLK, CT), F32),
            pltpu.VMEM((4, BLK, BLK), BF16),
            pltpu.VMEM((4, BLK, BLK), BF16),
            pltpu.VMEM((NZ, BLK, D), BF16),
            pltpu.VMEM((NZ, BLK, D), BF16),
            pltpu.VMEM((NZ, BLK, D), F32),
            pltpu.VMEM((2, 4, BLK, D), BF16),
            pltpu.VMEM((2, 4, BLK, D), BF16),
            pltpu.SemaphoreType.DMA((MESSAGES,)),
            pltpu.SemaphoreType.DMA((MESSAGES,)),
            pltpu.SemaphoreType.DMA((2,)),
        ],
        compiler_params=pltpu.CompilerParams(
            collective_id=0, has_side_effects=True, vmem_limit_bytes=60 << 20
        ),
        name="ranker",
    )(features, shortlist.T, positives.T, cluster_sizes, weights.reshape(8, BLK, D))
    return feature_grad, weight_grad.reshape(8 * BLK, BLK)


def solution(mesh):
    return jax.shard_map(
        local,
        mesh=mesh,
        in_specs=(
            P(("seq", "clus"), None),
            P(("seq", "clus"), None),
            P(("seq", "clus"), None),
            P("clus"),
            P("clus", None),
        ),
        out_specs=(P(("seq", "clus"), None), P("clus", "seq")),
        check_vma=False,
    )
```

```python
import math

import jax
import jax.numpy as jnp
from jax import lax
from jax.experimental import pallas as pl
from jax.experimental.pallas import tpu as pltpu
from jax.sharding import PartitionSpec as P

MESH = pl.DeviceIdType.MESH
NX, NY, NZ = 4, 4, 8
BLK = 128
SLOTS = 16
NB = 16
NK = 16
D = 1024
CT = 256
F32, BF16 = jnp.float32, jnp.bfloat16


ORDER = (
    "p0", "q0", "wb", "m1", "f10", "f11", "wo", "wn", "f12", "f13", "w1", "p1", "wm", "m2", "q1", "f20", "ws",
    "f21", "f22", "f23", "w2", "wt", "p2", "m3", "q2", "f30", "f31", "wp", "f32", "f33", "p3", "m4", "q3", "f40",
    "f41", "p4", "q4", "r0", "r2", "r1", "r3", "ds3", "ds2", "ds4", "ds7", "b0", "ds6", "ds1", "ds0", "b2", "lr2",
    "ds5", "lf2", "lf0", "lf7", "de3", "b1", "de2", "lf5", "lf6", "b3", "de4", "z10", "z11", "de7", "lr3", "lr6",
    "lf1", "lr8", "lr0", "lf8", "de6", "lr7", "lr5", "lr1", "lf3", "de1", "de0", "l27", "de5", "z22", "z23",
    "l22", "l25", "z20", "l20", "l26", "z21", "z32", "l21", "z33", "l28", "z30", "z31", "l23", "z42", "l32",
    "lf4", "l37", "lf9", "z43", "l30", "l35", "z40", "l31", "l36", "z41", "l33", "lr4", "l38", "lr9", "l29",
    "l24", "zf0", "zf3", "zf1", "zf2", "l34", "l39", "end",
)


def slot_of(dz, dc):
    hop = min(dz, NZ - dz)
    if hop == 0:
        return dc
    if hop == NZ // 2:
        return NB - 2 + dc
    return 4 * hop - 2 + (0 if dz < NZ // 2 else 1) + 2 * dc


def nt_dot(a, b):
    return lax.dot_general(a, b, (((1,), (1,)), ((), ())), preferred_element_type=F32)


def nn_dot(a, b):
    return jnp.dot(a, b, preferred_element_type=F32)


def body(
    scale, f_in, sl_in, pos_in, sz_in, w_in, df_out, wg_out,
    F, M, W, SZ, X, PGB, TG, PM, PT, SL, LP, RS, R1, R2, RB, RF, SB, SBR,
    DP, DS, EF, ZS, ZR, send_sems, recv_sems, local_sems,
):
    s, q = lax.axis_index("seq"), lax.axis_index("clus")
    x, c, y, z = s // 2, s % 2, q // NZ, q % NZ
    sib = (s + 1 - 2 * c, q)
    to_x = {1: ((s + 2) % 8, q), -1: ((s + 6) % 8, q)}
    to_y = {1: (s, (q + 8) % 32), -1: (s, (q + 24) % 32)}
    to_z = {1: (s, y * 8 + (z + 1) % 8), -1: (s, y * 8 + (z + 7) % 8)}
    partners = [sib, *to_x.values(), *to_y.values(), *to_z.values()]
    sent, arrived = [], set()

    def arrive(copy):
        if id(copy) not in arrived:
            arrived.add(id(copy))
            copy.wait_recv()

    def message(src, dst, device):
        number = len(sent)
        copy = pltpu.make_async_remote_copy(
            src_ref=src, dst_ref=dst, send_sem=send_sems.at[number], recv_sem=recv_sems.at[number],
            device_id=device, device_id_type=MESH,
        )
        copy.start()
        sent.append(copy)
        return copy

    cp_f = pltpu.make_async_copy(f_in, F.at[0], local_sems.at[0])
    cp_w = pltpu.make_async_copy(w_in.at[pl.ds(4 * c, 4)], W.at[0], local_sems.at[1])
    cp_f.start()
    cp_w.start()
    barrier = pltpu.get_barrier_semaphore()
    for device in partners:
        pl.semaphore_signal(barrier, inc=1, device_id=device, device_id_type=MESH)

    short = sl_in[...]
    place_row = lax.broadcasted_iota(jnp.int32, (16, BLK), 0)
    pos_cl = jnp.full((16, BLK), -1.0, F32)
    pos_off = jnp.full((16, BLK), -1.0, F32)
    for j in range(4):
        code = pos_in[j : j + 1, :]
        named = jnp.sum(jnp.where(place_row == (code >> 7), short, 0), axis=0, keepdims=True)
        pos_cl = jnp.where(place_row == j, named.astype(F32), pos_cl)
        pos_off = jnp.where(place_row == j, (code & 127).astype(F32), pos_off)
    M[0, 0:16, :] = short.astype(F32).astype(BF16)
    M[0, 16:32, :] = pos_cl.astype(BF16)
    M[0, 32:48, :] = pos_off.astype(BF16)
    row8 = lax.broadcasted_iota(jnp.int32, (8, BLK), 0)
    sizes = jnp.zeros((8, BLK), F32)
    for k in range(4):
        sizes = jnp.where(row8 == k, sz_in[4 * c + k].astype(F32), sizes)
    SZ[0] = sizes

    pl.semaphore_wait(barrier, len(partners))

    HALF = {"A": pl.ds(0, 64), "B": pl.ds(64, 64)}
    PIECE = [pl.ds(32 * p, 32) for p in range(4)]
    tasks = {}

    def landing(h, way):
        return h if way < 0 else NZ - h

    f_msg, m_msg, sf_msg, sm_msg = {}, {}, {}, {}

    def pieces(h, way):
        order = [0, 1, 2, 3] if way < 0 else [3, 2, 1, 0]
        return order[:2] if h == 4 else order

    def send_piece(h, way, p):
        src = slot_of(landing(h - 1, way) % NZ, 0)
        dst = slot_of(landing(h, way), 0)
        f_msg[h, way, p] = message(F.at[src, PIECE[p]], F.at[dst, PIECE[p]], to_z[way])

    def send_meta(h, way):
        src = slot_of(landing(h - 1, way) % NZ, 0)
        dst = slot_of(landing(h, way), 0)
        m_msg[h, way] = message(M.at[src], M.at[dst], to_z[way])

    def share_piece(dz, p):
        sf_msg[dz, p] = message(F.at[slot_of(dz, 0), PIECE[p]], F.at[slot_of(dz, 1), PIECE[p]], sib)

    def share_meta(dz):
        sm_msg[dz] = message(M.at[slot_of(dz, 0)], M.at[slot_of(dz, 1)], sib)

    def feature_step(h, i):
        for way in (-1, 1):
            p = pieces(h, way)[i]
            arrive(f_msg[h, way, p])
            if h < 4 and p in pieces(h + 1, way):
                send_piece(h + 1, way, p)
        for way in (-1, 1):
            share_piece(landing(h, way), pieces(h, way)[i])

    def meta_step(h):
        for way in (-1, 1):
            if h < 4 or way < 0:
                arrive(m_msg[h, way])
                if h < 3 or (h == 3 and way < 0):
                    send_meta(h + 1, way)
                share_meta(landing(h, way))

    w_msg, z_msg = {}, {}

    def near_weights(i, place, way):
        k = (x + i) % 4
        w_msg[place, i] = message(W.at[0, k], W.at[place, k], to_y[way])

    def opposite_weights():
        arrive(w_msg[1, "A"])
        w_msg["y", "A"] = message(W.at[1, x, HALF["A"]], W.at[2, x, HALF["A"]], to_y[-1])
        arrive(w_msg[3, "B"])
        w_msg["y", "B"] = message(W.at[3, x, HALF["B"]], W.at[2, x, HALF["B"]], to_y[1])
        arrive(z_msg[1])
        z_msg[2] = message(SZ.at[1], SZ.at[2], to_y[-1])

    def spread_weights():
        for first, way in (("A", -1), ("B", 1)):
            arrive(w_msg["y", first])
            w_msg["x", way, first] = message(W.at[2, x, HALF[first]], W.at[2, x, HALF[first]], to_x[way])

    def spread_rest():
        for second, way in (("B", -1), ("A", 1)):
            w_msg["x", way, second] = message(W.at[2, x, HALF[second]], W.at[2, x, HALF[second]], to_x[way])

    def pass_weights():
        for half, way, k in (("A", -1, (x + 1) % 4), ("B", 1, (x + 3) % 4)):
            arrive(w_msg["x", way, half])
            w_msg["xx", half] = message(W.at[2, k, HALF[half]], W.at[2, k, HALF[half]], to_x[way])

    def await_opposite():
        for half in ("A", "B"):
            arrive(w_msg["y", half])
            arrive(w_msg["x", -1, half])
            arrive(w_msg["x", 1, half])
            arrive(w_msg["xx", half])
        arrive(z_msg[2])

    def share_near(first):
        for place, way in ((1, 1), (3, -1)):
            half = ("A" if place == 1 else "B") if first else ("B" if place == 1 else "A")
            arrive(w_msg[place, half])
            w_msg["n", place, half] = message(
                W.at[place, x, HALF[half]], W.at[place, x, HALF[half]], to_x[way]
            )

    def await_near(place):
        for part in ("A", "B", *((1, 2) if place == 1 else (2, 3))):
            arrive(w_msg[place, part])
        arrive(w_msg["n", place, "A"])
        arrive(w_msg["n", place, "B"])
        arrive(z_msg[place])

    for way in (-1, 1):
        send_meta(1, way)
    share_meta(0)
    cp_f.wait()
    for i in range(4):
        for way in (-1, 1):
            send_piece(1, way, pieces(1, way)[i])
    sf_msg[0] = message(F.at[slot_of(0, 0)], F.at[slot_of(0, 1)], sib)
    z_msg[1] = message(SZ.at[0], SZ.at[1], to_y[-1])
    z_msg[3] = message(SZ.at[0], SZ.at[3], to_y[1])
    cp_w.wait()

    def first_weights(pair):
        for place, way, half in ((1, -1, pair[0]), (3, 1, pair[1])):
            w_msg[place, half] = message(W.at[0, x, HALF[half]], W.at[place, x, HALF[half]], to_y[way])

    first_weights("AB")

    kk16 = lax.broadcasted_iota(jnp.int32, (16, BLK), 0)
    cid16 = (((((y + (kk16 >> 2)) & 3) * 8 + z) * 8) + 4 * c + (kk16 & 3)).astype(F32)
    kk256 = lax.broadcasted_iota(jnp.int32, (256, 16), 0) >> 4
    cid256 = (((((y + (kk256 >> 2)) & 3) * 8 + z) * 8) + 4 * c + (kk256 & 3)).astype(F32)
    slot_row = lax.broadcasted_iota(jnp.int32, (16, BLK), 0).astype(F32)

    def pick(b):
        names = M[b, 0:16, :].astype(F32)
        member = jnp.zeros((16, BLK), F32)
        for j in range(16):
            member = member + jnp.where(names[j : j + 1, :] == cid16, 1.0, 0.0)
        before = (
            lax.broadcasted_iota(jnp.int32, (BLK, BLK), 0)
            < lax.broadcasted_iota(jnp.int32, (BLK, BLK), 1)
        )
        rank = nn_dot(member.astype(BF16), jnp.where(before, 1.0, 0.0).astype(BF16))
        rank = jnp.where(member > 0.0, rank, -1.0)
        for k in range(NK):
            PM[b, k * 16 : (k + 1) * 16, :] = jnp.where(
                rank[k : k + 1, :] == slot_row, 1.0, 0.0
            ).astype(BF16)
        picks = PM[b]
        PT[b] = jnp.transpose(picks.astype(F32)).astype(BF16)
        named = nt_dot(picks, M[b, 16:32, :])
        offset = nt_dot(picks, M[b, 32:48, :])
        TG[:, b] = jnp.where(named == cid256, offset, -1.0).reshape(16, 16, 16)
        for n in range(D // CT):
            cols = slice(n * CT, (n + 1) * CT)
            X[:, b, :, cols] = nn_dot(picks, F[b, :, cols]).astype(BF16).reshape(16, 16, CT)

    def pick_range(first, count):
        lax.fori_loop(0, count, lambda i, _: (pick(first + i), 0)[1], 0, unroll=count)

    def await_shared(dz):
        arrive(sm_msg[dz])
        if dz:
            for p in range(4):
                arrive(sf_msg[dz, p])
        else:
            arrive(sf_msg[0])

    def pick_shared(h):
        for dz in {h, (NZ - h) % NZ}:
            await_shared(dz)
        if h == 0:
            pick_range(1, 1)
        elif h == 4:
            pick_range(15, 1)
        else:
            pick_range(4 * h, 2)

    def pick_own(h):
        if h == 0:
            pick_range(0, 1)
        elif h == 4:
            pick_range(14, 1)
        else:
            pick_range(4 * h - 2, 2)

    for h in range(5):
        tasks[f"p{h}"] = lambda h=h: pick_own(h)
        tasks[f"q{h}"] = lambda h=h: pick_shared(h)
    for h in range(1, 5):
        tasks[f"m{h}"] = lambda h=h: meta_step(h)
        for i in range(len(pieces(h, 1))):
            tasks[f"f{h}{i}"] = lambda h=h, i=i: feature_step(h, i)
    tasks["wo"], tasks["ws"], tasks["wp"] = opposite_weights, spread_weights, pass_weights
    tasks["wn"], tasks["wm"] = lambda: share_near(True), lambda: share_near(False)
    tasks["wb"], tasks["wt"] = lambda: first_weights("BA"), spread_rest
    tasks["w1"] = lambda: (near_weights(1, 1, -1), near_weights(2, 3, 1))
    tasks["w2"] = lambda: (near_weights(2, 1, -1), near_weights(3, 3, 1))

    lane = lax.broadcasted_iota(jnp.int32, (256, BLK), 1).astype(F32)

    def logits_of(dy, k):
        return nt_dot(X[4 * dy + k].reshape(256, D), W[dy, k])

    def cluster(dy, k, logits):
        kk = 4 * dy + k
        target = TG[kk].reshape(256, 16)
        positive = target[:, 0:1] == lane
        for j in range(1, 4):
            positive = positive | (target[:, j : j + 1] == lane)
        sign = jnp.where(positive, 1.0, -1.0)
        live = lane < SZ[dy, k : k + 1, :]
        slope = jnp.where(live, -2.0 * sign * jnp.maximum(1.0 - sign * logits, 0.0), 0.0)
        slope = slope.astype(BF16)
        SL[kk] = slope
        for n in range(D // CT):
            cols = slice(n * CT, (n + 1) * CT)
            PGB[:, kk, :, cols] = nn_dot(slope, W[dy, k, :, cols]).astype(BF16).reshape(16, 16, CT)

    def label_part(dy, k):
        kk = 4 * dy + k
        turned = jnp.transpose(SL[kk].astype(F32)).astype(BF16)
        for dx in range(NX):
            cols = pl.ds(pl.multiple_of(CT * ((x + dx) % NX), CT), CT)
            part = nn_dot(turned, X[kk, :, :, cols].reshape(256, CT))
            LP[dx, dy, k] = part.astype(BF16)

    def clusters(dy):
        ahead = logits_of(dy, 0)
        for k in range(4):
            logits, ahead = ahead, logits_of(dy, k + 1) if k < 3 else None
            cluster(dy, k, logits)

    def label_parts(dy):
        for k in range(4):
            label_part(dy, k)

    def await_weights(dy):
        if dy == 2:
            await_opposite()
        elif dy:
            await_near(dy)

    def slopes(dy):
        await_weights(dy)
        clusters(dy)

    for i in range(NY):
        tasks[f"r{i}"] = lambda i=i: slopes(i)
        tasks[f"b{i}"] = lambda i=i: label_parts(i)

    class Ring:
        def __init__(self, number, to, part, own):
            self.number, self.to, self.part, self.own = number, to, part, own
            self.msg = {}

        def far(self):
            n = self.number
            self.msg["far", 0] = message(self.part(2, 0), R1.at[n, 0], self.to[1])
            self.msg["far", 1] = message(self.part(2, 1), R1.at[n, 1], self.to[-1])

        def raw(self):
            n = self.number
            self.msg["raw", 0] = message(self.part(1, 1), R2.at[n, 0, 1], self.to[1])
            self.msg["raw", 1] = message(self.part(3, 0), R2.at[n, 1, 0], self.to[-1])

        def second(self):
            n = self.number
            for i, rel, way in ((0, 1, 1), (1, 3, -1)):
                arrive(self.msg["far", i])
                RS[n, i] = (self.part(rel, i)[...].astype(F32) + R1[n, i].astype(F32)).astype(BF16)
                self.msg["sum", i] = message(RS.at[n, i], R2.at[n, i, i], self.to[way])

        def last(self, half):
            n = self.number
            arrive(self.msg["raw" if half else "sum", 0])
            arrive(self.msg["sum" if half else "raw", 1])
            return self.own(half) + R2[n, 0, half].astype(F32) + R2[n, 1, half].astype(F32)

    def own_part(dx, dy, k):
        return LP[dx, dy, k].astype(F32)

    low_x = [
        Ring(dy, to_x, lambda dx, h, dy=dy: LP.at[dx, dy, h], lambda h, dy=dy: own_part(0, dy, h))
        for dy in range(NY)
    ]
    low_y = Ring(4, to_y, lambda dy, h: RB.at[0, dy, h], lambda h: RF[0, h])
    high_y = [
        Ring(5 + dx, to_y, lambda dy, h, dx=dx: LP.at[dx, dy, 2 + h], lambda h, dx=dx: own_part(dx, 0, 2 + h))
        for dx in range(NX)
    ]
    high_x = Ring(9, to_x, lambda dx, h: RB.at[1, dx, h], lambda h: RF[1, h])

    def settle(ring, group, place):
        for half in range(2):
            total = ring.last(half)
            if place:
                RB[group, place, half] = total.astype(BF16)
            else:
                RF[group, half] = total

    own = {}

    def finish(ring, group):
        for half in range(2):
            k = 2 * group + half
            total = ring.last(half) * scale
            left, right = total[:, 0:128], total[:, 128:256]
            SB[k] = jnp.where(c == 0, right, left).astype(BF16)
            wg_out[4 * c + k] = jnp.where(c == 0, left, right).astype(BF16)
        own[group] = message(SB.at[pl.ds(2 * group, 2)], SBR.at[pl.ds(2 * group, 2)], sib)

    def put_back(b, store):
        for n in range(D // CT):
            cols = slice(n * CT, (n + 1) * CT)
            store(cols, nn_dot(PT[b], PGB[b, :, :, cols].reshape(256, CT)))

    d_msg, e_msg = {}, {}

    def for_sibling(dz):
        def store(cols, value):
            DP[dz, :, cols] = value.astype(BF16)

        put_back(slot_of(dz, 1), store)
        d_msg[dz] = message(DP.at[dz], DS.at[dz], sib)

    def for_self(dz):
        arrive(d_msg[dz])

        def store(cols, value):
            EF[dz, :, cols] = value + DS[dz, :, cols].astype(F32)

        put_back(slot_of(dz, 0), store)

    def z_place(t, way):
        return (5 - t) if way > 0 else (NZ - 5 + t) % NZ

    def z_send(t, way, p):
        lane_of = 0 if way > 0 else 1
        value = EF[z_place(t, way), PIECE[p], :]
        if (t - 1, way, p) in e_msg:
            arrive(e_msg[t - 1, way, p])
            value = value + ZR[lane_of, t - 2, PIECE[p], :].astype(F32)
        ZS[lane_of, t - 1, PIECE[p], :] = value.astype(BF16)
        e_msg[t, way, p] = message(
            ZS.at[lane_of, t - 1, PIECE[p]], ZR.at[lane_of, t - 1, PIECE[p]], to_z[way]
        )

    def z_step(t, p):
        z_send(t, 1, p)
        z_send(t, -1, 3 - p)

    def z_final(p):
        arrive(e_msg[4, 1, p])
        arrive(e_msg[4, -1, p])
        rows = PIECE[p]
        df_out[rows, :] = (
            EF[0, rows, :] + ZR[0, 3, rows, :].astype(F32) + ZR[1, 3, rows, :].astype(F32)
        ).astype(BF16)

    def end():
        for group in range(2):
            arrive(own[group])
        wg_out[pl.ds(4 * (1 - c), 4)] = SBR[...]

    for dz in range(NZ):
        tasks[f"ds{dz}"] = lambda dz=dz: for_sibling(dz)
        tasks[f"de{dz}"] = lambda dz=dz: for_self(dz)
    for p in range(4):
        for t in range(1 if p < 2 else 2, 5):
            tasks[f"z{t}{p}"] = lambda t=t, p=p: z_step(t, p)
        tasks[f"zf{p}"] = lambda p=p: z_final(p)
    for n, ring in enumerate((*low_x, low_y, *high_y, high_x)):
        tasks[f"lf{n}"], tasks[f"lr{n}"], tasks[f"l2{n}"] = ring.far, ring.raw, ring.second
    for i in range(4):
        tasks[f"l3{i}"] = lambda i=i: settle(low_x[i], 0, i)
        tasks[f"l3{5 + i}"] = lambda i=i: settle(high_y[i], 1, i)
    tasks["l34"] = lambda: finish(low_y, 0)
    tasks["l39"] = lambda: finish(high_x, 1)
    tasks["end"] = end

    for name in ORDER:
        tasks.pop(name)()
    assert not tasks
    for copy in sent:
        copy.wait_send()


MESSAGES = 220


def local(features, shortlist, positives, cluster_sizes, weights):
    pairs_mean = features.shape[0] * lax.axis_size("seq") * shortlist.shape[1] // cluster_sizes.shape[0]
    vmem = pl.BlockSpec(memory_space=pltpu.VMEM)
    anywhere = pl.BlockSpec(memory_space=pl.ANY)

    def kernel(*refs):
        body(1.0 / math.sqrt(pairs_mean), *refs)

    feature_grad, weight_grad = pl.pallas_call(
        kernel,
        out_shape=(
            jax.ShapeDtypeStruct((BLK, D), BF16),
            jax.ShapeDtypeStruct((8, BLK, BLK), BF16),
        ),
        in_specs=[anywhere, vmem, vmem, pl.BlockSpec(memory_space=pltpu.SMEM), anywhere],
        out_specs=(vmem, vmem),
        scratch_shapes=[
            pltpu.VMEM((NB, BLK, D), BF16),
            pltpu.VMEM((NB, 48, BLK), BF16),
            pltpu.VMEM((NY, 4, BLK, D), BF16),
            pltpu.VMEM((NY, 8, BLK), F32),
            pltpu.VMEM((NK, NB, SLOTS, D), BF16),
            pltpu.VMEM((NB, NK, SLOTS, D), BF16),
            pltpu.VMEM((NK, NB, SLOTS, 16), F32),
            pltpu.VMEM((NB, 256, BLK), BF16),
            pltpu.VMEM((NB, BLK, 256), BF16),
            pltpu.VMEM((NK, 256, BLK), BF16),
            pltpu.VMEM((NX, NY, 4, BLK, CT), BF16),
            pltpu.VMEM((10, 2, BLK, CT), BF16),
            pltpu.VMEM((10, 2, BLK, CT), BF16),
            pltpu.VMEM((10, 2, 2, BLK, CT), BF16),
            pltpu.VMEM((2, 4, 2, BLK, CT), BF16),
            pltpu.VMEM((2, 2, BLK, CT), F32),
            pltpu.VMEM((4, BLK, BLK), BF16),
            pltpu.VMEM((4, BLK, BLK), BF16),
            pltpu.VMEM((NZ, BLK, D), BF16),
            pltpu.VMEM((NZ, BLK, D), BF16),
            pltpu.VMEM((NZ, BLK, D), F32),
            pltpu.VMEM((2, 4, BLK, D), BF16),
            pltpu.VMEM((2, 4, BLK, D), BF16),
            pltpu.SemaphoreType.DMA((MESSAGES,)),
            pltpu.SemaphoreType.DMA((MESSAGES,)),
            pltpu.SemaphoreType.DMA((2,)),
        ],
        compiler_params=pltpu.CompilerParams(
            collective_id=0, has_side_effects=True, vmem_limit_bytes=60 << 20
        ),
        name="ranker",
    )(features, shortlist.T, positives.T, cluster_sizes, weights.reshape(8, BLK, D))
    def hand_over(df_in, wg_in, df_out, wg_out):
        df_out[...] = df_in[...]
        wg_out[...] = wg_in[...]

    return pl.pallas_call(
        hand_over,
        out_shape=(
            jax.ShapeDtypeStruct((BLK, D), BF16),
            jax.ShapeDtypeStruct((8 * BLK, BLK), BF16),
        ),
        in_specs=[vmem, vmem],
        out_specs=(vmem, vmem),
        name="hand_over",
    )(feature_grad, weight_grad.reshape(8 * BLK, BLK))


def solution(mesh):
    return jax.shard_map(
        local,
        mesh=mesh,
        in_specs=(
            P(("seq", "clus"), None),
            P(("seq", "clus"), None),
            P(("seq", "clus"), None),
            P("clus"),
            P("clus", None),
        ),
        out_specs=(P(("seq", "clus"), None), P("clus", "seq")),
        check_vma=False,
    )
```

```python
import math

import jax
import jax.numpy as jnp
from jax import lax
from jax.experimental import pallas as pl
from jax.experimental.pallas import tpu as pltpu
from jax.sharding import PartitionSpec as P

MESH = pl.DeviceIdType.MESH
NX, NY, NZ = 4, 4, 8
BLK = 128
SLOTS = 16
NB = 16
NK = 16
D = 1024
CT = 256
F32, BF16 = jnp.float32, jnp.bfloat16


ORDER = (
    "p0", "q0", "wb", "m1", "f10", "f11", "wo", "wn", "f12", "f13", "w1", "p1", "wm", "m2", "q1", "f20", "ws",
    "f21", "f22", "f23", "w2", "wt", "p2", "m3", "q2", "f30", "f31", "wp", "f32", "f33", "p3", "m4", "q3", "f40",
    "f41", "p4", "q4", "r0", "r2", "r1", "r3", "ds3", "ds2", "ds4", "ds7", "b0", "ds6", "ds1", "ds0", "b2", "lr2",
    "ds5", "lf2", "lf0", "lf7", "de3", "b1", "de2", "lf5", "lf6", "b3", "de4", "z10", "z11", "de7", "lr3", "lr6",
    "lf1", "lr8", "lr0", "lf8", "de6", "lr7", "lr5", "lr1", "lf3", "de1", "de0", "l27", "de5", "z22", "z23",
    "l22", "l25", "z20", "l20", "l26", "z21", "z32", "l21", "z33", "l28", "z30", "z31", "l23", "z42", "l32",
    "lf4", "l37", "lf9", "z43", "l30", "l35", "z40", "l31", "l36", "z41", "l33", "lr4", "l38", "lr9", "l29",
    "l24", "zf0", "zf3", "zf1", "zf2", "l34", "l39", "end",
)


def slot_of(dz, dc):
    hop = min(dz, NZ - dz)
    if hop == 0:
        return dc
    if hop == NZ // 2:
        return NB - 2 + dc
    return 4 * hop - 2 + (0 if dz < NZ // 2 else 1) + 2 * dc


def nt_dot(a, b):
    return lax.dot_general(a, b, (((1,), (1,)), ((), ())), preferred_element_type=F32)


def nn_dot(a, b):
    return jnp.dot(a, b, preferred_element_type=F32)


def body(
    scale, f_in, sl_in, pos_in, sz_in, w_in, df_out, wg_out,
    F, M, W, SZ, X, PGB, TG, PM, PT, SL, LP, RS, R1, R2, RB, RF, SB, SBR,
    DP, DS, EF, ZS, ZR, send_sems, recv_sems, local_sems,
):
    s, q = lax.axis_index("seq"), lax.axis_index("clus")
    x, c, y, z = s // 2, s % 2, q // NZ, q % NZ
    sib = (s + 1 - 2 * c, q)
    to_x = {1: ((s + 2) % 8, q), -1: ((s + 6) % 8, q)}
    to_y = {1: (s, (q + 8) % 32), -1: (s, (q + 24) % 32)}
    to_z = {1: (s, y * 8 + (z + 1) % 8), -1: (s, y * 8 + (z + 7) % 8)}
    partners = [sib, *to_x.values(), *to_y.values(), *to_z.values()]
    sent, arrived = [], set()

    def arrive(copy):
        if id(copy) not in arrived:
            arrived.add(id(copy))
            copy.wait_recv()

    def message(src, dst, device):
        number = len(sent)
        copy = pltpu.make_async_remote_copy(
            src_ref=src, dst_ref=dst, send_sem=send_sems.at[number], recv_sem=recv_sems.at[number],
            device_id=device, device_id_type=MESH,
        )
        copy.start()
        sent.append(copy)
        return copy

    cp_f = pltpu.make_async_copy(f_in, F.at[0], local_sems.at[0])
    cp_w = pltpu.make_async_copy(w_in.at[pl.ds(4 * c, 4)], W.at[0], local_sems.at[1])
    cp_f.start()
    cp_w.start()
    barrier = pltpu.get_barrier_semaphore()
    for device in partners:
        pl.semaphore_signal(barrier, inc=1, device_id=device, device_id_type=MESH)

    short = sl_in[...]
    place_row = lax.broadcasted_iota(jnp.int32, (16, BLK), 0)
    pos_cl = jnp.full((16, BLK), -1.0, F32)
    pos_off = jnp.full((16, BLK), -1.0, F32)
    for j in range(4):
        code = pos_in[j : j + 1, :]
        named = jnp.sum(jnp.where(place_row == (code >> 7), short, 0), axis=0, keepdims=True)
        pos_cl = jnp.where(place_row == j, named.astype(F32), pos_cl)
        pos_off = jnp.where(place_row == j, (code & 127).astype(F32), pos_off)
    M[0, 0:16, :] = short.astype(F32).astype(BF16)
    M[0, 16:32, :] = pos_cl.astype(BF16)
    M[0, 32:48, :] = pos_off.astype(BF16)
    row8 = lax.broadcasted_iota(jnp.int32, (8, BLK), 0)
    sizes = jnp.zeros((8, BLK), F32)
    for k in range(4):
        sizes = jnp.where(row8 == k, sz_in[4 * c + k].astype(F32), sizes)
    SZ[0] = sizes

    pl.semaphore_wait(barrier, len(partners))

    HALF = {"A": pl.ds(0, 64), "B": pl.ds(64, 64)}
    PIECE = [pl.ds(32 * p, 32) for p in range(4)]
    tasks = {}

    def landing(h, way):
        return h if way < 0 else NZ - h

    f_msg, m_msg, sf_msg, sm_msg = {}, {}, {}, {}

    def pieces(h, way):
        order = [0, 1, 2, 3] if way < 0 else [3, 2, 1, 0]
        return order[:2] if h == 4 else order

    def send_piece(h, way, p):
        src = slot_of(landing(h - 1, way) % NZ, 0)
        dst = slot_of(landing(h, way), 0)
        f_msg[h, way, p] = message(F.at[src, PIECE[p]], F.at[dst, PIECE[p]], to_z[way])

    def send_meta(h, way):
        src = slot_of(landing(h - 1, way) % NZ, 0)
        dst = slot_of(landing(h, way), 0)
        m_msg[h, way] = message(M.at[src], M.at[dst], to_z[way])

    def share_piece(dz, p):
        sf_msg[dz, p] = message(F.at[slot_of(dz, 0), PIECE[p]], F.at[slot_of(dz, 1), PIECE[p]], sib)

    def share_meta(dz):
        sm_msg[dz] = message(M.at[slot_of(dz, 0)], M.at[slot_of(dz, 1)], sib)

    def feature_step(h, i):
        for way in (-1, 1):
            p = pieces(h, way)[i]
            arrive(f_msg[h, way, p])
            if h < 4 and p in pieces(h + 1, way):
                send_piece(h + 1, way, p)
        for way in (-1, 1):
            share_piece(landing(h, way), pieces(h, way)[i])

    def meta_step(h):
        for way in (-1, 1):
            if h < 4 or way < 0:
                arrive(m_msg[h, way])
                if h < 3 or (h == 3 and way < 0):
                    send_meta(h + 1, way)
                share_meta(landing(h, way))

    w_msg, z_msg = {}, {}

    def near_weights(i, place, way):
        k = (x + i) % 4
        w_msg[place, i] = message(W.at[0, k], W.at[place, k], to_y[way])

    def opposite_weights():
        arrive(w_msg[1, "A"])
        w_msg["y", "A"] = message(W.at[1, x, HALF["A"]], W.at[2, x, HALF["A"]], to_y[-1])
        arrive(w_msg[3, "B"])
        w_msg["y", "B"] = message(W.at[3, x, HALF["B"]], W.at[2, x, HALF["B"]], to_y[1])
        arrive(z_msg[1])
        z_msg[2] = message(SZ.at[1], SZ.at[2], to_y[-1])

    def spread_weights():
        for first, way in (("A", -1), ("B", 1)):
            arrive(w_msg["y", first])
            w_msg["x", way, first] = message(W.at[2, x, HALF[first]], W.at[2, x, HALF[first]], to_x[way])

    def spread_rest():
        for second, way in (("B", -1), ("A", 1)):
            w_msg["x", way, second] = message(W.at[2, x, HALF[second]], W.at[2, x, HALF[second]], to_x[way])

    def pass_weights():
        for half, way, k in (("A", -1, (x + 1) % 4), ("B", 1, (x + 3) % 4)):
            arrive(w_msg["x", way, half])
            w_msg["xx", half] = message(W.at[2, k, HALF[half]], W.at[2, k, HALF[half]], to_x[way])

    def await_opposite():
        for half in ("A", "B"):
            arrive(w_msg["y", half])
            arrive(w_msg["x", -1, half])
            arrive(w_msg["x", 1, half])
            arrive(w_msg["xx", half])
        arrive(z_msg[2])

    def share_near(first):
        for place, way in ((1, 1), (3, -1)):
            half = ("A" if place == 1 else "B") if first else ("B" if place == 1 else "A")
            arrive(w_msg[place, half])
            w_msg["n", place, half] = message(
                W.at[place, x, HALF[half]], W.at[place, x, HALF[half]], to_x[way]
            )

    def await_near(place):
        for part in ("A", "B", *((1, 2) if place == 1 else (2, 3))):
            arrive(w_msg[place, part])
        arrive(w_msg["n", place, "A"])
        arrive(w_msg["n", place, "B"])
        arrive(z_msg[place])

    for way in (-1, 1):
        send_meta(1, way)
    share_meta(0)
    cp_f.wait()
    for i in range(4):
        for way in (-1, 1):
            send_piece(1, way, pieces(1, way)[i])
    sf_msg[0] = message(F.at[slot_of(0, 0)], F.at[slot_of(0, 1)], sib)
    z_msg[1] = message(SZ.at[0], SZ.at[1], to_y[-1])
    z_msg[3] = message(SZ.at[0], SZ.at[3], to_y[1])
    cp_w.wait()

    def first_weights(pair):
        for place, way, half in ((1, -1, pair[0]), (3, 1, pair[1])):
            w_msg[place, half] = message(W.at[0, x, HALF[half]], W.at[place, x, HALF[half]], to_y[way])

    first_weights("AB")

    kk16 = lax.broadcasted_iota(jnp.int32, (16, BLK), 0)
    cid16 = (((((y + (kk16 >> 2)) & 3) * 8 + z) * 8) + 4 * c + (kk16 & 3)).astype(F32)
    kk256 = lax.broadcasted_iota(jnp.int32, (256, 16), 0) >> 4
    cid256 = (((((y + (kk256 >> 2)) & 3) * 8 + z) * 8) + 4 * c + (kk256 & 3)).astype(F32)
    slot_row = lax.broadcasted_iota(jnp.int32, (16, BLK), 0).astype(F32)

    def pick(b):
        names = M[b, 0:16, :].astype(F32)
        member = jnp.zeros((16, BLK), F32)
        for j in range(16):
            member = member + jnp.where(names[j : j + 1, :] == cid16, 1.0, 0.0)
        before = (
            lax.broadcasted_iota(jnp.int32, (BLK, BLK), 0)
            < lax.broadcasted_iota(jnp.int32, (BLK, BLK), 1)
        )
        rank = nn_dot(member.astype(BF16), jnp.where(before, 1.0, 0.0).astype(BF16))
        rank = jnp.where(member > 0.0, rank, -1.0)
        for k in range(NK):
            PM[b, k * 16 : (k + 1) * 16, :] = jnp.where(
                rank[k : k + 1, :] == slot_row, 1.0, 0.0
            ).astype(BF16)
        picks = PM[b]
        PT[b] = jnp.transpose(picks.astype(F32)).astype(BF16)
        named = nt_dot(picks, M[b, 16:32, :])
        offset = nt_dot(picks, M[b, 32:48, :])
        TG[:, b] = jnp.where(named == cid256, offset, -1.0).reshape(16, 16, 16)
        for n in range(D // CT):
            cols = slice(n * CT, (n + 1) * CT)
            X[:, b, :, cols] = nn_dot(picks, F[b, :, cols]).astype(BF16).reshape(16, 16, CT)

    def pick_range(first, count):
        lax.fori_loop(0, count, lambda i, _: (pick(first + i), 0)[1], 0, unroll=count)

    def await_shared(dz):
        arrive(sm_msg[dz])
        if dz:
            for p in range(4):
                arrive(sf_msg[dz, p])
        else:
            arrive(sf_msg[0])

    def pick_shared(h):
        for dz in {h, (NZ - h) % NZ}:
            await_shared(dz)
        if h == 0:
            pick_range(1, 1)
        elif h == 4:
            pick_range(15, 1)
        else:
            pick_range(4 * h, 2)

    def pick_own(h):
        if h == 0:
            pick_range(0, 1)
        elif h == 4:
            pick_range(14, 1)
        else:
            pick_range(4 * h - 2, 2)

    for h in range(5):
        tasks[f"p{h}"] = lambda h=h: pick_own(h)
        tasks[f"q{h}"] = lambda h=h: pick_shared(h)
    for h in range(1, 5):
        tasks[f"m{h}"] = lambda h=h: meta_step(h)
        for i in range(len(pieces(h, 1))):
            tasks[f"f{h}{i}"] = lambda h=h, i=i: feature_step(h, i)
    tasks["wo"], tasks["ws"], tasks["wp"] = opposite_weights, spread_weights, pass_weights
    tasks["wn"], tasks["wm"] = lambda: share_near(True), lambda: share_near(False)
    tasks["wb"], tasks["wt"] = lambda: first_weights("BA"), spread_rest
    tasks["w1"] = lambda: (near_weights(1, 1, -1), near_weights(2, 3, 1))
    tasks["w2"] = lambda: (near_weights(2, 1, -1), near_weights(3, 3, 1))

    lane = lax.broadcasted_iota(jnp.int32, (256, BLK), 1).astype(F32)

    def logits_of(dy, k):
        return nt_dot(X[4 * dy + k].reshape(256, D), W[dy, k])

    def cluster(dy, k, logits):
        kk = 4 * dy + k
        target = TG[kk].reshape(256, 16)
        positive = target[:, 0:1] == lane
        for j in range(1, 4):
            positive = positive | (target[:, j : j + 1] == lane)
        sign = jnp.where(positive, 1.0, -1.0)
        live = lane < SZ[dy, k : k + 1, :]
        slope = jnp.where(live, -2.0 * sign * jnp.maximum(1.0 - sign * logits, 0.0), 0.0)
        slope = slope.astype(BF16)
        SL[kk] = slope
        for n in range(D // CT):
            cols = slice(n * CT, (n + 1) * CT)
            PGB[:, kk, :, cols] = nn_dot(slope, W[dy, k, :, cols]).astype(BF16).reshape(16, 16, CT)

    def turned_slopes(dy, k):
        return jnp.transpose(SL[4 * dy + k].astype(F32)).astype(BF16)

    def label_part(dy, k, turned):
        kk = 4 * dy + k
        for dx in range(NX):
            cols = pl.ds(pl.multiple_of(CT * ((x + dx) % NX), CT), CT)
            part = nn_dot(turned, X[kk, :, :, cols].reshape(256, CT))
            LP[dx, dy, k] = part.astype(BF16)

    def clusters(dy):
        ahead = logits_of(dy, 0)
        for k in range(4):
            logits, ahead = ahead, logits_of(dy, k + 1) if k < 3 else None
            cluster(dy, k, logits)

    def label_parts(dy):
        ahead = turned_slopes(dy, 0)
        for k in range(4):
            turned, ahead = ahead, turned_slopes(dy, k + 1) if k < 3 else None
            label_part(dy, k, turned)

    def await_weights(dy):
        if dy == 2:
            await_opposite()
        elif dy:
            await_near(dy)

    def slopes(dy):
        await_weights(dy)
        clusters(dy)

    for i in range(NY):
        tasks[f"r{i}"] = lambda i=i: slopes(i)
        tasks[f"b{i}"] = lambda i=i: label_parts(i)

    class Ring:
        def __init__(self, number, to, part, own):
            self.number, self.to, self.part, self.own = number, to, part, own
            self.msg = {}

        def far(self):
            n = self.number
            self.msg["far", 0] = message(self.part(2, 0), R1.at[n, 0], self.to[1])
            self.msg["far", 1] = message(self.part(2, 1), R1.at[n, 1], self.to[-1])

        def raw(self):
            n = self.number
            self.msg["raw", 0] = message(self.part(1, 1), R2.at[n, 0, 1], self.to[1])
            self.msg["raw", 1] = message(self.part(3, 0), R2.at[n, 1, 0], self.to[-1])

        def second(self):
            n = self.number
            for i, rel, way in ((0, 1, 1), (1, 3, -1)):
                arrive(self.msg["far", i])
                RS[n, i] = (self.part(rel, i)[...].astype(F32) + R1[n, i].astype(F32)).astype(BF16)
                self.msg["sum", i] = message(RS.at[n, i], R2.at[n, i, i], self.to[way])

        def last(self, half):
            n = self.number
            arrive(self.msg["raw" if half else "sum", 0])
            arrive(self.msg["sum" if half else "raw", 1])
            return self.own(half) + R2[n, 0, half].astype(F32) + R2[n, 1, half].astype(F32)

    def own_part(dx, dy, k):
        return LP[dx, dy, k].astype(F32)

    low_x = [
        Ring(dy, to_x, lambda dx, h, dy=dy: LP.at[dx, dy, h], lambda h, dy=dy: own_part(0, dy, h))
        for dy in range(NY)
    ]
    low_y = Ring(4, to_y, lambda dy, h: RB.at[0, dy, h], lambda h: RF[0, h])
    high_y = [
        Ring(5 + dx, to_y, lambda dy, h, dx=dx: LP.at[dx, dy, 2 + h], lambda h, dx=dx: own_part(dx, 0, 2 + h))
        for dx in range(NX)
    ]
    high_x = Ring(9, to_x, lambda dx, h: RB.at[1, dx, h], lambda h: RF[1, h])

    def settle(ring, group, place):
        for half in range(2):
            total = ring.last(half)
            if place:
                RB[group, place, half] = total.astype(BF16)
            else:
                RF[group, half] = total

    own = {}

    def finish(ring, group):
        for half in range(2):
            k = 2 * group + half
            total = ring.last(half) * scale
            left, right = total[:, 0:128], total[:, 128:256]
            SB[k] = jnp.where(c == 0, right, left).astype(BF16)
            wg_out[4 * c + k] = jnp.where(c == 0, left, right).astype(BF16)
        own[group] = message(SB.at[pl.ds(2 * group, 2)], SBR.at[pl.ds(2 * group, 2)], sib)

    def put_back(b, store):
        for n in range(D // CT):
            cols = slice(n * CT, (n + 1) * CT)
            store(cols, nn_dot(PT[b], PGB[b, :, :, cols].reshape(256, CT)))

    d_msg, e_msg = {}, {}

    def for_sibling(dz):
        def store(cols, value):
            DP[dz, :, cols] = value.astype(BF16)

        put_back(slot_of(dz, 1), store)
        d_msg[dz] = message(DP.at[dz], DS.at[dz], sib)

    def for_self(dz):
        arrive(d_msg[dz])

        def store(cols, value):
            EF[dz, :, cols] = value + DS[dz, :, cols].astype(F32)

        put_back(slot_of(dz, 0), store)

    def z_place(t, way):
        return (5 - t) if way > 0 else (NZ - 5 + t) % NZ

    def z_send(t, way, p):
        lane_of = 0 if way > 0 else 1
        value = EF[z_place(t, way), PIECE[p], :]
        if (t - 1, way, p) in e_msg:
            arrive(e_msg[t - 1, way, p])
            value = value + ZR[lane_of, t - 2, PIECE[p], :].astype(F32)
        ZS[lane_of, t - 1, PIECE[p], :] = value.astype(BF16)
        e_msg[t, way, p] = message(
            ZS.at[lane_of, t - 1, PIECE[p]], ZR.at[lane_of, t - 1, PIECE[p]], to_z[way]
        )

    def z_step(t, p):
        z_send(t, 1, p)
        z_send(t, -1, 3 - p)

    def z_final(p):
        arrive(e_msg[4, 1, p])
        arrive(e_msg[4, -1, p])
        rows = PIECE[p]
        df_out[rows, :] = (
            EF[0, rows, :] + ZR[0, 3, rows, :].astype(F32) + ZR[1, 3, rows, :].astype(F32)
        ).astype(BF16)

    def end():
        for group in range(2):
            arrive(own[group])
        wg_out[pl.ds(4 * (1 - c), 4)] = SBR[...]

    for dz in range(NZ):
        tasks[f"ds{dz}"] = lambda dz=dz: for_sibling(dz)
        tasks[f"de{dz}"] = lambda dz=dz: for_self(dz)
    for p in range(4):
        for t in range(1 if p < 2 else 2, 5):
            tasks[f"z{t}{p}"] = lambda t=t, p=p: z_step(t, p)
        tasks[f"zf{p}"] = lambda p=p: z_final(p)
    for n, ring in enumerate((*low_x, low_y, *high_y, high_x)):
        tasks[f"lf{n}"], tasks[f"lr{n}"], tasks[f"l2{n}"] = ring.far, ring.raw, ring.second
    for i in range(4):
        tasks[f"l3{i}"] = lambda i=i: settle(low_x[i], 0, i)
        tasks[f"l3{5 + i}"] = lambda i=i: settle(high_y[i], 1, i)
    tasks["l34"] = lambda: finish(low_y, 0)
    tasks["l39"] = lambda: finish(high_x, 1)
    tasks["end"] = end

    for name in ORDER:
        tasks.pop(name)()
    assert not tasks
    for copy in sent:
        copy.wait_send()


MESSAGES = 220


def local(features, shortlist, positives, cluster_sizes, weights):
    pairs_mean = features.shape[0] * lax.axis_size("seq") * shortlist.shape[1] // cluster_sizes.shape[0]
    vmem = pl.BlockSpec(memory_space=pltpu.VMEM)
    anywhere = pl.BlockSpec(memory_space=pl.ANY)

    def kernel(*refs):
        body(1.0 / math.sqrt(pairs_mean), *refs)

    feature_grad, weight_grad = pl.pallas_call(
        kernel,
        out_shape=(
            jax.ShapeDtypeStruct((BLK, D), BF16),
            jax.ShapeDtypeStruct((8, BLK, BLK), BF16),
        ),
        in_specs=[anywhere, vmem, vmem, pl.BlockSpec(memory_space=pltpu.SMEM), anywhere],
        out_specs=(vmem, vmem),
        scratch_shapes=[
            pltpu.VMEM((NB, BLK, D), BF16),
            pltpu.VMEM((NB, 48, BLK), BF16),
            pltpu.VMEM((NY, 4, BLK, D), BF16),
            pltpu.VMEM((NY, 8, BLK), F32),
            pltpu.VMEM((NK, NB, SLOTS, D), BF16),
            pltpu.VMEM((NB, NK, SLOTS, D), BF16),
            pltpu.VMEM((NK, NB, SLOTS, 16), F32),
            pltpu.VMEM((NB, 256, BLK), BF16),
            pltpu.VMEM((NB, BLK, 256), BF16),
            pltpu.VMEM((NK, 256, BLK), BF16),
            pltpu.VMEM((NX, NY, 4, BLK, CT), BF16),
            pltpu.VMEM((10, 2, BLK, CT), BF16),
            pltpu.VMEM((10, 2, BLK, CT), BF16),
            pltpu.VMEM((10, 2, 2, BLK, CT), BF16),
            pltpu.VMEM((2, 4, 2, BLK, CT), BF16),
            pltpu.VMEM((2, 2, BLK, CT), F32),
            pltpu.VMEM((4, BLK, BLK), BF16),
            pltpu.VMEM((4, BLK, BLK), BF16),
            pltpu.VMEM((NZ, BLK, D), BF16),
            pltpu.VMEM((NZ, BLK, D), BF16),
            pltpu.VMEM((NZ, BLK, D), F32),
            pltpu.VMEM((2, 4, BLK, D), BF16),
            pltpu.VMEM((2, 4, BLK, D), BF16),
            pltpu.SemaphoreType.DMA((MESSAGES,)),
            pltpu.SemaphoreType.DMA((MESSAGES,)),
            pltpu.SemaphoreType.DMA((2,)),
        ],
        compiler_params=pltpu.CompilerParams(
            collective_id=0, has_side_effects=True, vmem_limit_bytes=60 << 20
        ),
        name="ranker",
    )(features, shortlist.T, positives.T, cluster_sizes, weights.reshape(8, BLK, D))
    def hand_over(df_in, wg_in, df_out, wg_out):
        df_out[...] = df_in[...]
        wg_out[...] = wg_in[...]

    return pl.pallas_call(
        hand_over,
        out_shape=(
            jax.ShapeDtypeStruct((BLK, D), BF16),
            jax.ShapeDtypeStruct((8 * BLK, BLK), BF16),
        ),
        grid=(2,),
        in_specs=[pl.BlockSpec((BLK // 2, D), lambda i: (i, 0)), pl.BlockSpec((4 * BLK, BLK), lambda i: (i, 0))],
        out_specs=(
            pl.BlockSpec((BLK // 2, D), lambda i: (i, 0)),
            pl.BlockSpec((4 * BLK, BLK), lambda i: (i, 0)),
        ),
        name="hand_over",
    )(feature_grad, weight_grad.reshape(8 * BLK, BLK))


def solution(mesh):
    return jax.shard_map(
        local,
        mesh=mesh,
        in_specs=(
            P(("seq", "clus"), None),
            P(("seq", "clus"), None),
            P(("seq", "clus"), None),
            P("clus"),
            P("clus", None),
        ),
        out_specs=(P(("seq", "clus"), None), P("clus", "seq")),
        check_vma=False,
    )
```
